32 devices in a mesh: dp: 4 (over y, core), tm: 8 (over z, x).
Axes of the slice: x: 2, y: 2, z: 4, core: 2. Of those that a mesh axis runs over, the one named last changes fastest.
Arguments:
- inputs: bfloat16 [16, 2048, 1024], P('dp', 'tm'), may hold values from -6 to 6
- cotangent: bfloat16 [16, 2048, 1024], P('dp', 'tm'), may hold values from -6 to 6
- lengths: int32 [16], P('dp'), may hold values from 512 to 2048, as said below
- first_up: bfloat16 [1024, 4096], P('tm'), may hold values from -0.1875 to 0.1875
- first_down: bfloat16 [4096, 1024], P('tm'), may hold values from -0.09375 to 0.09375
- joint_proj: bfloat16 [1024, 3072], P('tm'), may hold values from -0.1875 to 0.1875
- rel_proj: bfloat16 [1024, 1024], P('tm'), may hold values from -0.1875 to 0.1875
- merge_proj: bfloat16 [1024, 1024], P('tm'), may hold values from -2 to 2
- conv_wide: bfloat16 [1024, 2048], P('tm'), may hold values from -0.1875 to 0.1875
- conv_narrow: bfloat16 [1024, 1024], P('tm'), may hold values from -0.1875 to 0.1875
- second_up: bfloat16 [1024, 4096], P('tm'), may hold values from -0.1875 to 0.1875
- second_down: bfloat16 [4096, 1024], P('tm'), may hold values from -0.09375 to 0.09375
- norm_gains: bfloat16 [6, 1024], P(None, 'tm'), may hold values from 0.5 to 1.5
- norm_shifts: bfloat16 [6, 1024], P(None, 'tm'), may hold values from -1 to 1
- pos_biases: bfloat16 [2, 1024], P(None, 'tm'), may hold values from -3 to 3
- depth_taps: bfloat16 [5, 1024], P(None, 'tm'), may hold values from -2.5 to 2.5
Outputs:
- output: bfloat16 [16, 2048, 1024], P('dp', 'tm')
- grad_inputs: bfloat16 [16, 2048, 1024], P('dp', 'tm')
- grad_first_up: float32 [1024, 4096], P('tm')
- grad_first_down: float32 [4096, 1024], P('tm')
- grad_joint_proj: float32 [1024, 3072], P('tm')
- grad_rel_proj: float32 [1024, 1024], P('tm')
- grad_merge_proj: float32 [1024, 1024], P('tm')
- grad_conv_wide: float32 [1024, 2048], P('tm')
- grad_conv_narrow: float32 [1024, 1024], P('tm')
- grad_second_up: float32 [1024, 4096], P('tm')
- grad_second_down: float32 [4096, 1024], P('tm')
- grad_norm_gains: float32 [6, 1024], P(None, 'tm')
- grad_norm_shifts: float32 [6, 1024], P(None, 'tm')
- grad_pos_biases: float32 [2, 1024], P(None, 'tm')
- grad_depth_taps: float32 [5, 1024], P(None, 'tm')
The draws below stay inside these ranges and needn't reach their ends.
Inputs may be any that keep to these rules, and one draw needn't show every extreme that they name: `lengths`: in each group of 4 consecutive utterances the longest possible length grows with the group's index; the first utterance has 512 frames and the last 2048.
All inputs are finite; a program needn't handle non-finite values.
Results may differ from the reference program's by a relative error of at most 0.024.
Values may be sent and summed in bfloat16 or wider, within the bound.
No kernel may reach another device: no remote copies, remote signals or barrier semaphores. Data moves between devices by JAX's collectives and lax.ppermute only.
A program may use at most 384 MiB of HBM per device.

```python
import math
import jax
import jax.numpy as jnp
from jax import lax

D = 1024
FF = 4096
HEADS = 8
HEAD_DIM = 128
KW = 5
SLOT = 2048
UTT = 4
UTTS = 16


def draw_lengths(key, part):
    low_end = SLOT // 4
    group_index = jnp.arange(UTTS, dtype=jnp.int32) // UTT
    groups = UTTS // UTT
    high_end = low_end + (group_index + 1) * (SLOT - low_end) // groups
    picked = jax.random.randint(key, (UTTS,), low_end, high_end + 1, dtype=jnp.int32)
    picked = picked.at[0].set(low_end)
    return picked.at[UTTS - 1].set(SLOT)


def level_of(own_key, shape, cuts, low, top_value):
    def one(axis_at, parts):
        steps = jax.random.uniform(jax.random.fold_in(jax.random.fold_in(own_key, 6), axis_at), (parts,), jnp.float32, low / len(cuts), top_value / len(cuts))
        return jnp.repeat(jnp.exp(steps), shape[axis_at] // parts).reshape((-1,) + (1,) * (len(shape) - axis_at - 1))

    gain = one(*cuts[0])
    for cut in cuts[1:]:
        gain = gain * one(*cut)
    return gain


def bell_draw(stream_key, dims, deviation, reach, cuts=(), kind=jnp.bfloat16):
    values = deviation * jax.random.normal(stream_key, dims, jnp.float32)
    if cuts:
        values = values * level_of(stream_key, dims, cuts, -0.22, 0.18)
    return jnp.clip(values, -reach, reach).astype(kind)


def setup_inputs(seed: int = 0) -> dict:
    seeds = jax.random.split(jax.random.key(seed), 17)
    inputs = bell_draw(seeds[0], (UTTS, SLOT, D), 1.0, 6.0, ((0, 4), (1, 8)))
    cotangent = bell_draw(seeds[1], (UTTS, SLOT, D), 1.0, 6.0, ((0, 4), (1, 8)))
    lengths = draw_lengths(jax.random.fold_in(seeds[16], 71), 0)
    first_up = bell_draw(seeds[3], (D, FF), D ** -0.5, 0.1875, ((0, 8),))
    first_down = bell_draw(seeds[4], (FF, D), FF ** -0.5, 0.09375, ((0, 8),))
    joint_proj = bell_draw(seeds[5], (D, 3 * D), D ** -0.5, 0.1875, ((0, 8),))
    rel_proj = bell_draw(seeds[6], (D, D), D ** -0.5, 0.1875, ((0, 8),))
    merge_proj = bell_draw(seeds[7], (D, D), (max(1, D // 128)) ** -0.5, 2.0, ((0, 8),))
    conv_wide = bell_draw(seeds[8], (D, 2 * D), D ** -0.5, 0.1875, ((0, 8),))
    conv_narrow = bell_draw(seeds[9], (D, D), D ** -0.5, 0.1875, ((0, 8),))
    second_up = bell_draw(seeds[10], (D, FF), D ** -0.5, 0.1875, ((0, 8),))
    second_down = bell_draw(seeds[11], (FF, D), FF ** -0.5, 0.09375, ((0, 8),))
    norm_gains = jnp.clip(1.0 + 0.1 * jax.random.normal(seeds[12], (6, D), jnp.float32), 0.5, 1.5).astype(jnp.bfloat16)
    norm_shifts = bell_draw(seeds[13], (6, D), 0.2, 1.0, ((1, 8),))
    pos_biases = bell_draw(seeds[14], (2, D), 0.5, 3.0, ((1, 8),))
    depth_taps = bell_draw(seeds[15], (KW, D), KW ** -0.5, 2.5, ((1, 8),))
    return dict(inputs=inputs, cotangent=cotangent, lengths=lengths, first_up=first_up, first_down=first_down, joint_proj=joint_proj, rel_proj=rel_proj, merge_proj=merge_proj, conv_wide=conv_wide, conv_narrow=conv_narrow, second_up=second_up, second_down=second_down, norm_gains=norm_gains, norm_shifts=norm_shifts, pos_biases=pos_biases, depth_taps=depth_taps)


@jax.custom_vjp
def low(v):
    return lax.optimization_barrier(v.astype(jnp.bfloat16)).astype(jnp.float32)

@jax.custom_vjp
def low_back(v):
    return v

def low_keep(v):
    return (low(v), None)

def low_pass(kept, grad):
    return (grad,)

def back_keep(v):
    return (v, None)

def back_low(kept, grad):
    return (low(grad),)
low.defvjp(low_keep, low_pass)
low_back.defvjp(back_keep, back_low)
eps_norm = 1e-05
neg_fill = -1e+30

def matmul(left, right):
    return jnp.dot(left, right, precision=lax.Precision.HIGHEST, preferred_element_type=jnp.float32)

def layer_norm(values, gain_row, shift_row):
    mean_val = lax.optimization_barrier(jnp.mean(values, axis=-1, keepdims=True))
    centered = values - mean_val
    var_val = lax.optimization_barrier(jnp.mean(centered * centered, axis=-1, keepdims=True))
    return centered * lax.rsqrt(var_val + eps_norm) * gain_row + shift_row

def swish_act(values):
    return values * jax.nn.sigmoid(values)

def sinusoid(distance, feat_width):
    half_width = feat_width // 2
    inv_freq = jnp.exp(jnp.arange(half_width, dtype=jnp.float32) * (-2.0 * math.log(10000.0) / feat_width))
    angles = distance[:, None] * inv_freq[None, :]
    return jnp.concatenate([jnp.sin(angles), jnp.cos(angles)], axis=1)

def rel_shift(raw, key_count):
    lead_dims = raw.shape[:-2]
    row_count = raw.shape[-2]
    col_span = raw.shape[-1]
    flattened = raw.reshape(lead_dims + (row_count * col_span,))
    flattened = flattened[..., row_count - 1:row_count - 1 + row_count * (col_span - 1)]
    return flattened.reshape(lead_dims + (row_count, col_span - 1))[..., :key_count]

def attend_utterance(query_u, query_v, key_rows, value_rows, rel_rows, length):
    block_rows = min(512, SLOT)
    key_live = jnp.arange(SLOT, dtype=jnp.int32) < length
    keys_heads = key_rows.reshape(SLOT, HEADS, HEAD_DIM)
    values_heads = value_rows.reshape(SLOT, HEADS, HEAD_DIM)

    def query_block(block_start):
        part_u = lax.dynamic_slice_in_dim(query_u, block_start, block_rows, 0).reshape(block_rows, HEADS, HEAD_DIM)
        part_v = lax.dynamic_slice_in_dim(query_v, block_start, block_rows, 0).reshape(block_rows, HEADS, HEAD_DIM)
        window = lax.dynamic_slice_in_dim(rel_rows, SLOT - block_rows - block_start, block_rows + SLOT - 1, 0)
        window = window.reshape(block_rows + SLOT - 1, HEADS, HEAD_DIM)
        content = jnp.einsum('qhc,khc->hqk', part_u, keys_heads, precision=lax.Precision.HIGHEST)
        relative = rel_shift(jnp.einsum('qhc,whc->hqw', part_v, window, precision=lax.Precision.HIGHEST), SLOT)
        scores = low_back((content + relative) * HEAD_DIM ** (-0.5))
        scores = jnp.where(key_live[None, None, :], scores, neg_fill)
        softmaxed = jax.nn.softmax(scores, axis=-1)
        mixed = jnp.einsum('hqk,khc->qhc', low(softmaxed), values_heads, precision=lax.Precision.HIGHEST)
        return mixed.reshape(block_rows, D)
    starts = jnp.arange(SLOT // block_rows, dtype=jnp.int32) * block_rows
    return lax.map(jax.checkpoint(query_block), starts).reshape(SLOT, D)

def feed_forward(values, gain_row, shift_row, up_weight, down_weight):
    hidden = low_back(matmul(low(layer_norm(values, gain_row, shift_row)), up_weight))
    return low_back(matmul(low(swish_act(hidden)), down_weight))

def reference(inputs, cotangent, lengths, first_up, first_down, joint_proj, rel_proj, merge_proj, conv_wide, conv_narrow, second_up, second_down, norm_gains, norm_shifts, pos_biases, depth_taps):
    live_mask = (jnp.arange(SLOT, dtype=jnp.int32)[None, :] < lengths[:, None]).astype(jnp.float32)[:, :, None]
    distance = (SLOT - 1 - jnp.arange(2 * SLOT - 1, dtype=jnp.int32)).astype(jnp.float32)
    table_low = low(sinusoid(distance, D))
    pad_width = KW // 2

    def forward(section_zero, up_one, down_one, joint_w, rel_w, merge_w, wide_w, narrow_w, up_two, down_two, gain_rows, shift_rows, bias_rows, kernel_taps):
        flat_rows = section_zero.reshape(UTTS * SLOT, D)
        section_one = flat_rows + 0.5 * feed_forward(flat_rows, gain_rows[0], shift_rows[0], up_one, down_one)
        att_in = low(layer_norm(section_one, gain_rows[1], shift_rows[1]))
        joint_out = low_back(matmul(att_in, joint_w))
        query = joint_out[:, :D]
        query_u = low(query + bias_rows[0]).reshape(UTTS, SLOT, D)
        query_v = low(query + bias_rows[1]).reshape(UTTS, SLOT, D)
        key_rows = low(joint_out[:, D:2 * D]).reshape(UTTS, SLOT, D)
        value_rows = low(joint_out[:, 2 * D:]).reshape(UTTS, SLOT, D)
        rel_rows = low(matmul(table_low, rel_w))
        attended = lax.map(lambda mapped: attend_utterance(mapped[0], mapped[1], mapped[2], mapped[3], rel_rows, mapped[4]), (query_u, query_v, key_rows, value_rows, lengths))
        attended = low_back(attended.reshape(UTTS * SLOT, D))
        section_two = section_one + low_back(matmul(low(attended), merge_w))
        conv_in = low(layer_norm(section_two, gain_rows[2], shift_rows[2]))
        wide_out = low_back(matmul(conv_in, wide_w))
        gated = (wide_out[:, :D] * jax.nn.sigmoid(wide_out[:, D:])).reshape(UTTS, SLOT, D) * live_mask
        framed = jnp.pad(gated, ((0, 0), (pad_width, pad_width), (0, 0)))
        depth_out = kernel_taps[0] * framed[:, 0:SLOT]
        for offset in range(1, KW):
            depth_out = depth_out + kernel_taps[offset] * framed[:, offset:offset + SLOT]
        frame_count = jnp.sum(live_mask)
        mean_val = lax.optimization_barrier(jnp.sum(depth_out * live_mask, axis=(0, 1))) / frame_count
        centered = depth_out - mean_val
        var_val = lax.optimization_barrier(jnp.sum(centered * centered * live_mask, axis=(0, 1))) / frame_count
        batch_normed = (centered * lax.rsqrt(var_val + eps_norm) * gain_rows[5] + shift_rows[5]).reshape(UTTS * SLOT, D)
        section_three = section_two + low_back(matmul(low(swish_act(batch_normed)), narrow_w))
        section_four = section_three + 0.5 * feed_forward(section_three, gain_rows[3], shift_rows[3], up_two, down_two)
        return layer_norm(section_four, gain_rows[4], shift_rows[4]).reshape(UTTS, SLOT, D)
    result, pullback = jax.vjp(forward, inputs.astype(jnp.float32), first_up.astype(jnp.float32), first_down.astype(jnp.float32), joint_proj.astype(jnp.float32), rel_proj.astype(jnp.float32), merge_proj.astype(jnp.float32), conv_wide.astype(jnp.float32), conv_narrow.astype(jnp.float32), second_up.astype(jnp.float32), second_down.astype(jnp.float32), norm_gains.astype(jnp.float32), norm_shifts.astype(jnp.float32), pos_biases.astype(jnp.float32), depth_taps.astype(jnp.float32))
    gradients = pullback(cotangent.astype(jnp.float32))
    return (result.astype(jnp.bfloat16), gradients[0].astype(jnp.bfloat16), gradients[1], gradients[2], gradients[3], gradients[4], gradients[5], gradients[6], gradients[7], gradients[8], gradients[9], gradients[10], gradients[11], gradients[12], gradients[13])
```

```python
import functools
import math

import jax
import jax.numpy as jnp
from jax import lax
from jax.experimental import pallas as pl
from jax.experimental.pallas import tpu as pltpu
from jax.sharding import PartitionSpec as P

D = 1024
HEADS = 8
HEAD_DIM = 128
KW = 5

AXES = ("dp", "tm")
LOG2E = math.log2(math.e)
eps_norm = 1e-05
neg_fill = -1e30
f32 = jnp.float32
bf16 = jnp.bfloat16


def product(left, right):
    return jnp.dot(left, right, preferred_element_type=f32)


def product_nt(left, right):
    return lax.dot_general(left, right, (((1,), (1,)), ((), ())), preferred_element_type=f32)


def product_tn(left, right):
    return lax.dot_general(left, right, (((0,), (0,)), ((), ())), preferred_element_type=f32)


def tile_start(own, tile_at, rows, tile):
    per = rows // tile
    return ((tile_at // per) ^ own) * rows + (tile_at % per) * tile


def biased_queries(q_ref, bias_ref):
    query = q_ref[0].astype(f32)
    scale = HEAD_DIM**-0.5 * LOG2E
    query_u = ((query + bias_ref[0:1, :]) * scale).astype(bf16)
    query_v = ((query + bias_ref[1:2, :]) * scale).astype(bf16)
    return query_u, query_v


def slot_scores(query_u, query_v, key, rel_window, mask_row, rows, tile):
    width = rows + tile
    raw = product_nt(query_v, rel_window)
    shifted = pltpu.roll(raw, width - (tile - 1), 1, stride=1, stride_axis=0)[:, :rows]
    return shifted + product_nt(query_u, key) + mask_row


def attend_kernel(
    own_ref, q_ref, k_ref, v_ref, rel_ref, bias_ref, mask_ref, out_ref, lse_ref, score_ref,
    *, slots, rows, tile
):
    own = own_ref[0]
    start = tile_start(own, pl.program_id(1), rows, tile)
    query_u, query_v = biased_queries(q_ref, bias_ref)
    top = jnp.full((tile, 1), -jnp.inf, f32)
    for s in range(slots):
        base = pl.multiple_of(slots * rows - tile - start + (own ^ s) * rows, tile)
        scores = slot_scores(
            query_u, query_v, k_ref[s], rel_ref[pl.ds(base, rows + tile), :],
            mask_ref[0:1, s * rows : (s + 1) * rows], rows, tile,
        )
        score_ref[s] = scores
        top = jnp.maximum(top, jnp.max(scores, axis=1, keepdims=True))
    total = jnp.zeros((tile, 1), f32)
    mixed = jnp.zeros((tile, HEAD_DIM), f32)
    for s in range(slots):
        weights = jnp.exp2(score_ref[s] - top)
        total = total + jnp.sum(weights, axis=1, keepdims=True)
        mixed = mixed + product(weights.astype(bf16), v_ref[s])
    out_ref[0] = (mixed / total).astype(bf16)
    lse_ref[0] = top + jnp.log2(total)


def attend_back_kernel(
    own_ref, q_ref, k_ref, v_ref, rel_ref, bias_ref, mask_ref, o_ref, do_ref, lse_ref,
    dq_ref, dk_ref, dv_ref, drel_ref, dbias_ref, dk_acc, dv_acc, *, slots, rows, tile
):
    own = own_ref[0]
    tile_at = pl.program_id(1)
    start = tile_start(own, tile_at, rows, tile)
    scale = HEAD_DIM**-0.5

    @pl.when(tile_at == 0)
    def _():
        dk_acc[...] = jnp.zeros_like(dk_acc)
        dv_acc[...] = jnp.zeros_like(dv_acc)
        drel_ref[...] = jnp.zeros_like(drel_ref)
        dbias_ref[...] = jnp.zeros_like(dbias_ref)

    query_u, query_v = biased_queries(q_ref, bias_ref)
    grad_out = do_ref[0]
    inner = jnp.sum(grad_out.astype(f32) * o_ref[0].astype(f32), axis=1, keepdims=True)
    lse = lse_ref[0]
    width = rows + tile
    row_at = lax.broadcasted_iota(jnp.int32, (tile, tile), 0)
    col_at = lax.broadcasted_iota(jnp.int32, (tile, tile), 1)
    flip = (row_at + col_at == tile - 1).astype(bf16)
    query_v_flip = product(flip, query_v).astype(bf16)
    grad_u = jnp.zeros((tile, HEAD_DIM), f32)
    grad_v_flip = jnp.zeros((tile, HEAD_DIM), f32)
    for s in range(slots):
        base = pl.multiple_of(slots * rows - tile - start + (own ^ s) * rows, tile)
        rel_window = rel_ref[pl.ds(base, width), :]
        key = k_ref[s]
        scores = slot_scores(
            query_u, query_v, key, rel_window, mask_ref[0:1, s * rows : (s + 1) * rows], rows, tile
        )
        probs = jnp.exp2(scores - lse)
        grad_probs = product_nt(grad_out, v_ref[s])
        grad_scores = (probs * (grad_probs - inner)).astype(bf16)
        dv_acc[s] += product_tn(probs.astype(bf16), grad_out)
        dk_acc[s] += product_tn(grad_scores, query_u)
        grad_u = grad_u + product(grad_scores, key)
        flipped = product(flip, grad_scores).astype(bf16)
        padded = jnp.concatenate([flipped, jnp.zeros((tile, width - rows), bf16)], axis=1)
        grad_raw = pltpu.roll(padded, 0, 1, stride=1, stride_axis=0)
        grad_v_flip = grad_v_flip + product(grad_raw, rel_window)
        drel_ref[pl.ds(base, width), :] += product_tn(grad_raw, query_v_flip)
    high = grad_v_flip.astype(bf16)
    low = (grad_v_flip - high.astype(f32)).astype(bf16)
    grad_v = product(flip, high) + product(flip, low)
    dbias_ref[0, 0:1, :] += jnp.sum(grad_u, axis=0, keepdims=True) * scale
    dbias_ref[0, 1:2, :] += jnp.sum(grad_v, axis=0, keepdims=True) * scale
    dq_ref[0] = ((grad_u + grad_v) * scale).astype(bf16)

    @pl.when(tile_at == pl.num_programs(1) - 1)
    def _():
        dk_ref[...] = (dk_acc[...] * (1.0 / LOG2E)).astype(bf16)
        dv_ref[...] = dv_acc[...].astype(bf16)
        drel_ref[...] = drel_ref[...] * (1.0 / LOG2E)


def attention_specs(slots, rows, heads, tile):
    per = rows // tile
    span = slots * rows
    by_tile = pl.BlockSpec((1, tile, HEAD_DIM), lambda h, i, own: (i // per, i % per, h))
    in_specs = [
        by_tile,
        pl.BlockSpec((slots, rows, HEAD_DIM), lambda h, i, own: (0, 0, heads + h)),
        pl.BlockSpec((slots, rows, HEAD_DIM), lambda h, i, own: (0, 0, 2 * heads + h)),
        pl.BlockSpec((2 * span, HEAD_DIM), lambda h, i, own: (0, h)),
        pl.BlockSpec((2, HEAD_DIM), lambda h, i, own: (0, h)),
        pl.BlockSpec((1, span), lambda h, i, own: (0, 0)),
    ]
    return (heads, slots * per), by_tile, in_specs


def attend(own, joint, rel, bias, mask):
    slots, rows, wide = joint.shape
    heads = wide // (3 * HEAD_DIM)
    span, tile = slots * rows, min(256, rows)
    grid, by_tile, in_specs = attention_specs(slots, rows, heads, tile)
    return pl.pallas_call(
        functools.partial(attend_kernel, slots=slots, rows=rows, tile=tile),
        grid_spec=pltpu.PrefetchScalarGridSpec(
            num_scalar_prefetch=1,
            grid=grid,
            in_specs=in_specs,
            out_specs=[by_tile, pl.BlockSpec((1, tile, 1), lambda h, i, own: (h, i, 0))],
            scratch_shapes=[pltpu.VMEM((slots, tile, rows), f32)],
        ),
        out_shape=[
            jax.ShapeDtypeStruct((slots, rows, heads * HEAD_DIM), bf16),
            jax.ShapeDtypeStruct((heads, span, 1), f32),
        ],
        compiler_params=pltpu.CompilerParams(vmem_limit_bytes=56 << 20),
        cost_estimate=pl.CostEstimate(
            flops=heads * span * span * HEAD_DIM * 8,
            bytes_accessed=heads * span * HEAD_DIM * 20,
            transcendentals=heads * span * span,
        ),
        name="attend",
    )(own, joint, joint, joint, rel, bias, mask)


def attend_back(own, joint, rel, bias, mask, out, grad_out, lse):
    slots, rows, wide = joint.shape
    heads = wide // (3 * HEAD_DIM)
    span, tile = slots * rows, min(256, rows)
    grid, by_tile, in_specs = attention_specs(slots, rows, heads, tile)
    by_head = pl.BlockSpec((slots, rows, HEAD_DIM), lambda h, i, own: (0, 0, h))
    return pl.pallas_call(
        functools.partial(attend_back_kernel, slots=slots, rows=rows, tile=tile),
        grid_spec=pltpu.PrefetchScalarGridSpec(
            num_scalar_prefetch=1,
            grid=grid,
            in_specs=in_specs
            + [by_tile, by_tile, pl.BlockSpec((1, tile, 1), lambda h, i, own: (h, i, 0))],
            out_specs=[
                by_tile,
                by_head,
                by_head,
                pl.BlockSpec((2 * span, HEAD_DIM), lambda h, i, own: (0, h)),
                pl.BlockSpec((1, 2, HEAD_DIM), lambda h, i, own: (h, 0, 0)),
            ],
            scratch_shapes=[pltpu.VMEM((slots, rows, HEAD_DIM), f32)] * 2,
        ),
        out_shape=[jax.ShapeDtypeStruct((slots, rows, heads * HEAD_DIM), bf16)] * 3
        + [
            jax.ShapeDtypeStruct((2 * span, heads * HEAD_DIM), f32),
            jax.ShapeDtypeStruct((heads, 2, HEAD_DIM), f32),
        ],
        compiler_params=pltpu.CompilerParams(vmem_limit_bytes=56 << 20),
        cost_estimate=pl.CostEstimate(
            flops=heads * span * span * HEAD_DIM * 22,
            bytes_accessed=heads * span * HEAD_DIM * 40,
            transcendentals=heads * span * span,
        ),
        name="attend_back",
    )(own, joint, joint, joint, rel, bias, mask, out, grad_out, lse)


def norm_fwd(values, gain_row, shift_row):
    centered = values - jnp.mean(values, axis=-1, keepdims=True)
    scale_inv = lax.rsqrt(jnp.mean(centered * centered, axis=-1, keepdims=True) + eps_norm)
    normal = centered * scale_inv
    return (normal * gain_row + shift_row, normal, scale_inv)


def norm_back(grad_out, normal, scale_inv, gain_row):
    grad_norm = grad_out * gain_row
    grad_in = scale_inv * (
        grad_norm
        - jnp.mean(grad_norm, axis=-1, keepdims=True)
        - normal * jnp.mean(grad_norm * normal, axis=-1, keepdims=True)
    )
    return (grad_in, jnp.sum(grad_out * normal, axis=0), jnp.sum(grad_out, axis=0))


def swish_grad(values):
    sigmoid_val = jax.nn.sigmoid(values)
    return sigmoid_val * (1.0 + values * (1.0 - sigmoid_val))


def sinusoid(distance, feat_width):
    half_width = feat_width // 2
    inv_freq = jnp.exp(jnp.arange(half_width, dtype=f32) * (-2.0 * math.log(10000.0) / feat_width))
    angles = distance[:, None] * inv_freq[None, :]
    return jnp.concatenate([jnp.sin(angles), jnp.cos(angles)], axis=1)


class Layout:
    def __init__(self, utt_count):
        self.dp, self.tm, self.utt = lax.axis_size("dp"), lax.axis_size("tm"), utt_count
        self.pairs = self.dp // 2
        self.size = self.tm // utt_count
        self.subs = self.size // 2
        dp_at, t = lax.axis_index("dp"), lax.axis_index("tm")
        self.core, self.t = dp_at % 2, t
        group, self.sub = t // self.subs, t % self.subs
        self.home_core, self.home_slot = group % 2, group // 2
        self.own = self.core * self.subs + self.sub

    def route(self, target):
        pairs = []
        for p in range(self.pairs):
            for c in range(2):
                for t in range(self.tm):
                    tp, tc, tt = target(p, c, t)
                    pairs.append(((2 * p + c) * self.tm + t, (2 * tp + tc) * self.tm + tt))
        return pairs

    def send(self, values, target):
        return lax.ppermute(values, AXES, self.route(target))

    def to_class(self, step):
        def target(p, c, t):
            other = (c * self.subs + t % self.subs) ^ step
            return p, other // self.subs, t - t % self.subs + other % self.subs

        return target

    def to_core(self, p, c, t):
        return p, 1 - c, t

    def home(self, step):
        def target(p, c, t):
            kind, at = t // self.utt, t % self.utt
            place = (step + at) % self.utt
            return p, kind // self.subs, (2 * place + c) * self.subs + kind % self.subs

        return target

    def enter(self, shard):
        at = self.t % self.utt
        result = jnp.zeros_like(shard)
        for k in range(self.utt):
            block = lax.dynamic_index_in_dim(shard, (k + at) % self.utt, 0, keepdims=True)
            block = self.send(block, self.home(k))
            result = lax.dynamic_update_slice_in_dim(
                result, block, (self.home_slot - k) % self.utt, axis=0
            )
        return result

    def leave(self, blocks):
        at = self.t % self.utt
        result = jnp.zeros_like(blocks)
        for k in range(self.utt):
            block = lax.dynamic_index_in_dim(
                blocks, (self.home_slot - k) % self.utt, 0, keepdims=True
            )
            there = self.route(self.home(k))
            block = lax.ppermute(block, AXES, [(b, a) for a, b in there])
            result = lax.dynamic_update_slice_in_dim(result, block, (k + at) % self.utt, axis=0)
        return result

    def all_slots(self, values):
        parts = [values] + [self.send(values, self.to_class(s)) for s in range(1, self.size)]
        return jnp.concatenate(parts, axis=0)

    def own_sum(self, partial):
        parts = partial.reshape((self.size, -1) + partial.shape[1:])
        total = parts[0]
        for s in range(1, self.size):
            total = total + self.send(parts[s].astype(bf16), self.to_class(s)).astype(f32)
        return total

    def over_utterances(self, values, join):
        step = 1
        groups = 2 * self.utt
        while step < self.pairs * groups:

            def target(p, c, t, step=step):
                other = (p * groups + t // self.subs) ^ step
                return other // groups, c, (other % groups) * self.subs + t % self.subs

            values = join(values, self.send(values, target))
            step *= 2
        return values

    def core_half(self, values, axis):
        shape = values.shape
        split = values.reshape(shape[:axis] + (2, shape[axis] // 2) + shape[axis + 1 :])
        return lax.dynamic_index_in_dim(split, self.core, axis, keepdims=False)

    def sub_part(self, values, axis):
        if self.subs == 1:
            return values
        width = values.shape[axis] // self.subs
        return lax.dynamic_slice_in_dim(values, self.sub * width, width, axis)

    def sub_place(self, values, axis):
        if self.subs == 1:
            return values
        width = values.shape[axis]
        shape = list(values.shape)
        shape[axis] = width * self.subs
        return lax.dynamic_update_slice_in_dim(
            jnp.zeros(shape, values.dtype), values, self.sub * width, axis
        )

    def cols_half(self, local, groups):
        rows, cols = local.shape
        split = local.reshape(rows, groups, 2, cols // (2 * groups))
        return lax.dynamic_index_in_dim(split, self.core, 2, keepdims=False).reshape(rows, cols // 2)

    def cols_join(self, halves, groups):
        _, rows, cols = halves.shape
        split = halves.reshape(2, rows, groups, cols // groups)
        return split.transpose(1, 2, 0, 3).reshape(rows, 2 * cols)

    def gather_small(self, local):
        parts = local[None]
        step = 1
        while step < self.tm:
            parts = jnp.concatenate(
                [parts, self.send(parts, lambda p, c, t, step=step: (p, c, t ^ step))], axis=0
            )
            step *= 2
        parts = jnp.take(parts, jnp.arange(self.tm, dtype=jnp.int32) ^ self.t, axis=0)
        return parts.transpose(1, 0, 2).reshape(local.shape[0], -1)

    def sum_all(self, values):
        step = 1
        while step < self.size:
            values = values + self.send(values, self.to_class(step))
            step *= 2
        return self.over_utterances(values, jnp.add)

    def gather(self, locals_):
        plane = lax.axis_index("dp") // 2
        parts = [lax.dynamic_slice_in_dim(v, plane * (v.shape[0] // self.pairs), v.shape[0] // self.pairs, 0) for v in locals_]
        packed, places = pack(parts)
        groups = [
            [(2 * p + c) * self.tm + t for t in range(self.tm) for p in range(self.pairs)]
            for c in range(2)
        ]
        full = lax.all_gather(packed[None], AXES, axis=0, tiled=True, axis_index_groups=groups)
        return [v.reshape(-1, v.shape[-1]) for v in unpack(full, places)]

    def scatter(self, grads, over_planes=False, after=None):
        plane = lax.axis_index("dp") // 2
        split = [g.astype(bf16).reshape(self.tm, self.pairs, -1, g.shape[-1]) for g in grads]

        def part(at):
            return pack([lax.dynamic_index_in_dim(v, at, 1, keepdims=False) for v in split])

        mine, places = part(plane)
        if over_planes:
            for s in range(1, self.pairs):
                other = self.send(part(plane ^ s)[0], lambda p, c, t, s=s: (p ^ s, c, t))
                mine = (mine.astype(f32) + other.astype(f32)).astype(bf16)
        else:
            mine = jnp.stack([part(plane ^ s)[0] for s in range(self.pairs)], axis=1)
        if after is not None:
            mine, _ = lax.optimization_barrier((mine, after))
        return lax.psum_scatter(mine, "tm", scatter_dimension=0, tiled=True), places

    def collect(self, mine, places):
        plane = lax.axis_index("dp") // 2
        if mine.ndim == 4:
            parts = mine
            mine = parts[:, 0].astype(f32)
            for s in range(1, self.pairs):
                mine = mine + self.send(parts[:, s], lambda p, c, t, s=s: (p ^ s, c, t)).astype(f32)
            mine = mine.astype(bf16)
        whole = jnp.zeros((self.pairs,) + mine.shape[1:], bf16)
        whole = lax.dynamic_update_slice_in_dim(whole, mine, plane, 0)
        for s in range(1, self.pairs):
            other = self.send(mine, lambda p, c, t, s=s: (p ^ s, c, t))
            whole = lax.dynamic_update_slice_in_dim(whole, other, plane ^ s, 0)
        there = self.send(whole, self.to_core)
        both = jnp.stack(
            [jnp.where(self.core == 0, whole, there), jnp.where(self.core == 0, there, whole)]
        )
        return [v.astype(f32).reshape(2, -1, v.shape[-1]) for v in unpack(both, places)]


def pack(parts):
    blocks, places, row, spare = [], [], 0, None
    for v in parts:
        rows, cols, own = v.shape[-2], v.shape[-1], []
        for at in range(0, cols - D + 1, D):
            blocks.append([v[..., at : at + D]])
            own.append((row, 0, rows, D))
            row += rows
        if cols % D:
            piece = v[..., cols - cols % D :]
            if spare is not None and spare[1] == rows and spare[2] + cols % D <= D:
                blocks[spare[0]].append(piece)
                own.append((spare[3], spare[2], rows, cols % D))
                spare = None
            else:
                spare = (len(blocks), rows, cols % D, row)
                blocks.append([piece])
                own.append((row, 0, rows, cols % D))
                row += rows
        places.append(own)
    filled = []
    for block in blocks:
        joined = block[0] if len(block) == 1 else jnp.concatenate(block, axis=-1)
        if joined.shape[-1] < D:
            pads = [(0, 0)] * (joined.ndim - 1) + [(0, D - joined.shape[-1])]
            joined = jnp.pad(joined, pads)
        filled.append(joined)
    return jnp.concatenate(filled, axis=-2), places


def unpack(packed, places):
    results = []
    for own in places:
        pieces = [packed[..., r : r + n, c : c + m] for r, c, n, m in own]
        results.append(pieces[0] if len(pieces) == 1 else jnp.concatenate(pieces, axis=-1))
    return results


def merge_moments(left, right):
    count_a, mean_a, square_a = left[0], left[1], left[2]
    count_b, mean_b, square_b = right[0], right[1], right[2]
    count = count_a + count_b
    gap = mean_a - mean_b
    mean = (count_a * mean_a + count_b * mean_b) / count
    square = (square_a + square_b) + gap * gap * (count_a * count_b / count)
    return jnp.stack([count, mean, square])


def body(
    inputs,
    cotangent,
    lengths,
    first_up,
    first_down,
    joint_proj,
    rel_proj,
    merge_proj,
    conv_wide,
    conv_narrow,
    second_up,
    second_down,
    norm_gains,
    norm_shifts,
    pos_biases,
    depth_taps,
):
    lay = Layout(inputs.shape[0])
    utt_count, block_len, _ = inputs.shape
    tm, size, own = lay.tm, lay.size, lay.own
    rows = utt_count * block_len
    span = rows * size
    feats = D // size
    pad_width = KW // 2

    small = jnp.concatenate([norm_gains, norm_shifts, pos_biases, depth_taps], axis=0)
    small = lay.gather_small(small).astype(f32)
    gain_rows, shift_rows = small[0:6], small[6:12]

    def own_feats(values):
        count = values.shape[0]
        split = values.reshape(count, tm, 2, D // (2 * tm))
        half = lax.dynamic_index_in_dim(split, lay.core, 2, keepdims=False)
        return lay.sub_part(half.reshape(count, D // 2), 1)

    def place_feats(values):
        count = values.shape[0]
        half = lay.sub_place(values, 1).reshape(count, tm, 1, D // (2 * tm))
        pick = (jnp.arange(2) == lay.core).astype(f32)[None, None, :, None]
        return (half * pick).reshape(count, D)

    def place_heads(values):
        return lax.dynamic_update_slice_in_dim(
            jnp.zeros((values.shape[0], D), f32), values, own * feats, axis=1
        )

    bias_rows = lax.dynamic_slice_in_dim(small[12:14], own * feats, feats, axis=1)
    kernel_taps = own_feats(small[14 : 14 + KW])
    batch_gain, batch_shift = own_feats(gain_rows[5:6])[0], own_feats(shift_rows[5:6])[0]

    up_one, down_one = lay.gather([lay.cols_half(first_up, tm), lay.core_half(first_down, 0)])
    joint_half, rel_half = lay.gather([lay.cols_half(joint_proj, 3), lay.cols_half(rel_proj, 1)])
    merge_full, wide_half, narrow_half = lay.gather(
        [merge_proj, lay.cols_half(conv_wide, 2 * tm), lay.core_half(conv_narrow, 0)]
    )
    up_two, down_two = lay.gather([lay.cols_half(second_up, tm), lay.core_half(second_down, 0)])
    up_one, down_one = lay.sub_part(up_one, 1), lay.sub_part(down_one, 0)
    up_two, down_two = lay.sub_part(up_two, 1), lay.sub_part(down_two, 0)
    joint_own = lay.sub_part(joint_half.reshape(D, 3, D // 2), 2).reshape(D, 3 * feats)
    rel_own = lay.sub_part(rel_half, 1)
    wide_own = lay.sub_part(wide_half.reshape(D, 2, D // 2), 2).reshape(D, 2 * feats)
    narrow_own = lay.sub_part(narrow_half, 0)
    merge_slots = jnp.concatenate(
        [
            lax.dynamic_slice_in_dim(merge_full, (own ^ s) * feats, feats, axis=0)
            for s in range(size)
        ],
        axis=0,
    )

    def feed_forward(values, gain_row, shift_row, up_weight, down_weight):
        normed, normal, scale_inv = norm_fwd(values, gain_row, shift_row)
        normed_low = lay.all_slots(normed.astype(bf16))
        hidden = product(normed_low, up_weight)
        active_low = (hidden * jax.nn.sigmoid(hidden)).astype(bf16)
        result = lay.own_sum(product(active_low, down_weight))
        return (result, (normal, scale_inv, normed_low, hidden, active_low))

    def feed_back(grad_result, saved_acts, gain_row, up_weight, down_weight, between):
        normal, scale_inv, normed_low, hidden, active_low = saved_acts
        grad_low = lay.all_slots(grad_result.astype(bf16))
        grad_down = product_tn(active_low, grad_low).astype(bf16)
        grad_down, grad_low = lax.optimization_barrier((grad_down, grad_low))
        grad_hidden = (product_nt(grad_low, down_weight) * swish_grad(hidden)).astype(bf16)
        grad_up = product_tn(normed_low, grad_hidden).astype(bf16)
        grad_down, grad_up = lay.sub_place(grad_down, 0), lay.sub_place(grad_up, 1)
        grad_hidden, moved = between(grad_down, grad_up, grad_hidden)
        grad_values, grad_gain, grad_shift = norm_back(
            lay.own_sum(product_nt(grad_hidden, up_weight)), normal, scale_inv, gain_row
        )
        return (grad_values, moved, grad_gain, grad_shift)

    group_lengths = jnp.where(
        lay.home_core == lay.core, lengths, lay.send(lengths, lay.to_core)
    )
    length = lax.dynamic_index_in_dim(group_lengths, lay.home_slot, 0, keepdims=False)
    slot_class = jnp.arange(size, dtype=jnp.int32) ^ own
    frame_pos = slot_class[:, None] * rows + jnp.arange(rows, dtype=jnp.int32)[None, :]
    live = frame_pos < length
    live_col = live.astype(f32)[:, :, None]
    key_mask = jnp.where(live, 0.0, neg_fill).astype(f32).reshape(1, span)
    own_at = own.reshape(1).astype(jnp.int32)

    def framed_rows(values):
        last, leading = values[:, rows - pad_width :], values[:, :pad_width]
        before, after = [], []
        for s in range(size):
            kind = own ^ s
            prev = lax.dynamic_index_in_dim(last, jnp.maximum(kind - 1, 0) ^ own, 0)
            following = lax.dynamic_index_in_dim(
                leading, jnp.minimum(kind + 1, size - 1) ^ own, 0
            )
            before.append(jnp.where(kind > 0, prev, 0.0))
            after.append(jnp.where(kind < size - 1, following, 0.0))
        return jnp.concatenate(
            [jnp.concatenate(before, axis=0), values, jnp.concatenate(after, axis=0)], axis=1
        )

    distance = (span - 1 - jnp.arange(2 * span, dtype=jnp.int32)).astype(f32)
    table_low = sinusoid(distance, D).astype(bf16)
    up_one, table_low = lax.optimization_barrier((up_one, table_low))
    section_zero = lay.enter(inputs).astype(f32).reshape(rows, D)
    branch_one, saved_one = feed_forward(
        section_zero, gain_rows[0], shift_rows[0], up_one, down_one
    )
    section_one = section_zero + 0.5 * branch_one
    att_normed, att_normal, att_inv = norm_fwd(section_one, gain_rows[1], shift_rows[1])
    att_low = lay.all_slots(att_normed.astype(bf16))
    joint_out = product(att_low, joint_own).astype(bf16).reshape(size, rows, 3 * feats)
    rel_low = product(table_low, rel_own).astype(bf16)
    attended, log_totals = attend(own_at, joint_out, rel_low, bias_rows, key_mask)
    attended_low = jnp.concatenate(
        [attended[0]] + [lay.send(attended[s], lay.to_class(s)) for s in range(1, size)], axis=1
    )
    section_two = section_one + product(attended_low, merge_slots)
    conv_normed, conv_normal, conv_inv = norm_fwd(section_two, gain_rows[2], shift_rows[2])
    conv_low = lay.all_slots(conv_normed.astype(bf16))
    wide_out = product(conv_low, wide_own).reshape(size, rows, 2 * feats)
    lin_half = wide_out[:, :, :feats]
    gate_sig = jax.nn.sigmoid(wide_out[:, :, feats:])
    gated = lin_half * gate_sig * live_col
    framed = framed_rows(gated)
    depth_out = kernel_taps[0] * framed[:, 0:rows]
    for offset in range(1, KW):
        depth_out = depth_out + kernel_taps[offset] * framed[:, offset : offset + rows]
    own_count = length.astype(f32)
    own_mean = jnp.sum(depth_out * live_col, axis=(0, 1)) / own_count
    own_gap = (depth_out - own_mean) * live_col
    moments = jnp.stack(
        [jnp.broadcast_to(own_count, (feats,)), own_mean, jnp.sum(own_gap * own_gap, axis=(0, 1))]
    )
    total_count, bn_mean, total_var = lay.over_utterances(moments, merge_moments)
    bn_inv = lax.rsqrt(total_var / total_count + eps_norm)
    bn_normal = (depth_out - bn_mean) * bn_inv
    bn_flat = bn_normal * batch_gain + batch_shift
    swish_low = (bn_flat * jax.nn.sigmoid(bn_flat)).astype(bf16).reshape(span, feats)
    section_three = section_two + lay.own_sum(product(swish_low, narrow_own))
    section_three, cotangent = lax.optimization_barrier((section_three, cotangent))
    grad_entry = lay.enter(cotangent)
    branch_four, saved_four = feed_forward(
        section_three, gain_rows[3], shift_rows[3], up_two, down_two
    )
    section_four = section_three + 0.5 * branch_four
    final_out, final_normal, final_inv = norm_fwd(section_four, gain_rows[4], shift_rows[4])
    output = lay.leave(final_out.astype(bf16).reshape(utt_count, block_len, D))

    grad_final = grad_entry.astype(f32).reshape(rows, D)
    grad_four, gain_four, shift_four = norm_back(grad_final, final_normal, final_inv, gain_rows[4])

    def scatter_two(grad_down, grad_up, grad_hidden):
        moved = lay.scatter([grad_up, grad_down])
        return grad_hidden, moved

    grad_mid, moved_two, gain_three, shift_three = feed_back(
        0.5 * grad_four, saved_four, gain_rows[3], up_two, down_two, scatter_two
    )
    grad_three = grad_four + grad_mid
    narrow_low = lay.all_slots(grad_three.astype(bf16))
    grad_narrow = lay.sub_place(product_tn(swish_low, narrow_low), 0)
    grad_batch = product_nt(narrow_low, narrow_own).reshape(size, rows, feats) * swish_grad(bn_flat)
    gain_batch = jnp.sum(grad_batch * bn_normal, axis=(0, 1))
    shift_batch = jnp.sum(grad_batch, axis=(0, 1))
    grad_hat = grad_batch * batch_gain
    total_hat, total_cross = lay.over_utterances(
        jnp.stack([shift_batch * batch_gain, gain_batch * batch_gain]), jnp.add
    )
    grad_depth = bn_inv * (
        grad_hat - live_col / total_count * (total_hat + bn_normal * total_cross)
    )
    grad_framed = framed_rows(grad_depth)
    grad_gated = kernel_taps[0] * grad_framed[:, KW - 1 : KW - 1 + rows]
    for offset in range(1, KW):
        grad_gated = (
            grad_gated + kernel_taps[offset] * grad_framed[:, KW - 1 - offset : KW - 1 - offset + rows]
        )
    grad_taps = jnp.stack(
        [
            jnp.sum(grad_depth * framed[:, offset : offset + rows], axis=(0, 1))
            for offset in range(KW)
        ]
    )
    grad_glu = grad_gated * live_col
    grad_wide_out = (
        jnp.concatenate(
            [grad_glu * gate_sig, grad_glu * lin_half * gate_sig * (1.0 - gate_sig)], axis=2
        )
        .astype(bf16)
        .reshape(span, 2 * feats)
    )
    grad_wide = lay.sub_place(product_tn(conv_low, grad_wide_out).reshape(D, 2, feats), 2)
    grad_conv_in, gain_two, shift_two = norm_back(
        lay.own_sum(product_nt(grad_wide_out, wide_own)), conv_normal, conv_inv, gain_rows[2]
    )
    grad_two = grad_three + grad_conv_in
    merge_low, output = lax.optimization_barrier((grad_two.astype(bf16), output))
    grad_merge = product_tn(attended_low, merge_low).astype(bf16)
    grad_merge = jnp.concatenate(
        [
            lax.dynamic_slice_in_dim(grad_merge, (own ^ s) * feats, feats, axis=0)
            for s in range(size)
        ],
        axis=0,
    )
    halves = grad_merge.reshape(D, 2, D // 2)
    mine = lax.dynamic_index_in_dim(halves, lay.core, 1, keepdims=False)
    theirs = lax.dynamic_index_in_dim(halves, 1 - lay.core, 1, keepdims=False)
    grad_merge = mine.astype(f32) + lay.send(theirs, lay.to_core).astype(f32)
    grad_attended = product_nt(merge_low, merge_slots).astype(bf16).reshape(rows, size, feats)
    grad_attended = jnp.stack(
        [grad_attended[:, 0]]
        + [lay.send(grad_attended[:, s], lay.to_class(s)) for s in range(1, size)]
    )
    grad_attended, rows_two = lax.optimization_barrier((grad_attended, moved_two[0]))
    moved_conv = lay.scatter([grad_merge, grad_wide.reshape(D, D), grad_narrow], after=rows_two)
    grad_query, grad_key, grad_value, grad_rel, grad_biases = attend_back(
        own_at, joint_out, rel_low, bias_rows, key_mask, attended, grad_attended, log_totals
    )
    grad_query, rows_conv = lax.optimization_barrier((grad_query, moved_conv[0]))
    grad_biases = grad_biases.transpose(1, 0, 2).reshape(2, feats)
    rel_high = grad_rel.astype(bf16)
    rel_rest = (grad_rel - rel_high.astype(f32)).astype(bf16)
    grad_rel_proj = lay.sub_place(
        product_tn(table_low, rel_high) + product_tn(table_low, rel_rest), 1
    )
    grad_joint_out = jnp.concatenate([grad_query, grad_key, grad_value], axis=2).reshape(
        span, 3 * feats
    )
    grad_joint = lay.sub_place(product_tn(att_low, grad_joint_out).reshape(D, 3, feats), 2)
    grad_att_in, gain_one, shift_one = norm_back(
        lay.own_sum(product_nt(grad_joint_out, joint_own)), att_normal, att_inv, gain_rows[1]
    )
    grad_one = grad_two + grad_att_in
    moved_joint = lay.scatter(
        [grad_joint.reshape(D, 3 * D // 2), grad_rel_proj], over_planes=True, after=rows_conv
    )

    def scatter_one(grad_down, grad_up, grad_hidden):
        grad_hidden, rows_joint = lax.optimization_barrier((grad_hidden, moved_joint[0]))
        moved_down = lay.scatter([grad_down], after=rows_joint)
        moved_up = lay.scatter([grad_up], over_planes=True, after=moved_down[0])
        return grad_hidden, (moved_down, moved_up)

    grad_first, (moved_down, moved_up), gain_zero, shift_zero = feed_back(
        0.5 * grad_one, saved_one, gain_rows[0], up_one, down_one, scatter_one
    )
    grad_zero = grad_one + grad_first
    grad_inputs = lay.leave(grad_zero.astype(bf16).reshape(utt_count, block_len, D))

    summed_up_two, summed_down_two = lay.collect(rows_two, moved_two[1])
    summed_merge, summed_wide, summed_narrow = lay.collect(rows_conv, moved_conv[1])
    summed_joint, summed_rel = lay.collect(*moved_joint)
    (summed_down_one,) = lay.collect(*moved_down)
    (summed_up_one,) = lay.collect(*moved_up)
    summed_up_one = lay.cols_join(summed_up_one, tm)
    summed_up_two = lay.cols_join(summed_up_two, tm)
    summed_joint = lay.cols_join(summed_joint, 3)
    summed_rel = lay.cols_join(summed_rel, 1)
    summed_merge = lay.cols_join(summed_merge, 1)
    summed_wide = lay.cols_join(summed_wide, 2 * tm)
    summed_down_one = summed_down_one.reshape(-1, D)
    summed_down_two = summed_down_two.reshape(-1, D)
    summed_narrow = summed_narrow.reshape(-1, D)

    small_grads = jnp.concatenate(
        [
            jnp.stack([gain_zero, gain_one, gain_two, gain_three, gain_four]),
            place_feats(gain_batch[None]),
            jnp.stack([shift_zero, shift_one, shift_two, shift_three, shift_four]),
            place_feats(shift_batch[None]),
            place_heads(grad_biases),
            place_feats(grad_taps),
        ],
        axis=0,
    )
    small_grads = lay.sum_all(small_grads)
    small_grads = lax.dynamic_slice_in_dim(small_grads, lay.t * (D // tm), D // tm, axis=1)
    return (
        output,
        grad_inputs,
        summed_up_one,
        summed_down_one,
        summed_joint,
        summed_rel,
        summed_merge,
        summed_wide,
        summed_narrow,
        summed_up_two,
        summed_down_two,
        small_grads[0:6],
        small_grads[6:12],
        small_grads[12:14],
        small_grads[14 : 14 + KW],
    )


def solution(mesh):
    frames = P("dp", "tm", None)
    rows, cols = P("tm", None), P(None, "tm")
    return jax.shard_map(
        body,
        mesh=mesh,
        in_specs=(frames, frames, P("dp")) + (rows,) * 9 + (cols,) * 4,
        out_specs=(frames, frames) + (rows,) * 9 + (cols,) * 4,
        check_vma=False,
    )
```

```python
import functools
import math

import jax
import jax.numpy as jnp
from jax import lax
from jax.experimental import pallas as pl
from jax.experimental.pallas import tpu as pltpu
from jax.sharding import PartitionSpec as P

D = 1024
HEADS = 8
HEAD_DIM = 128
KW = 5

AXES = ("dp", "tm")
LOG2E = math.log2(math.e)
eps_norm = 1e-05
neg_fill = -1e30
f32 = jnp.float32
bf16 = jnp.bfloat16


def product(left, right):
    return jnp.dot(left, right, preferred_element_type=f32)


def product_nt(left, right):
    return lax.dot_general(left, right, (((1,), (1,)), ((), ())), preferred_element_type=f32)


def product_tn(left, right):
    return lax.dot_general(left, right, (((0,), (0,)), ((), ())), preferred_element_type=f32)


def tile_start(own, tile_at, rows, tile):
    per = rows // tile
    return ((tile_at // per) ^ own) * rows + (tile_at % per) * tile


def biased_queries(q_ref, bias_ref):
    query = q_ref[0].astype(f32)
    scale = HEAD_DIM**-0.5 * LOG2E
    query_u = ((query + bias_ref[0:1, :]) * scale).astype(bf16)
    query_v = ((query + bias_ref[1:2, :]) * scale).astype(bf16)
    return query_u, query_v


def slot_scores(query_u, query_v, key, rel_window, mask_row, rows, tile):
    width = rows + tile
    raw = product_nt(query_v, rel_window)
    shifted = pltpu.roll(raw, width - (tile - 1), 1, stride=1, stride_axis=0)[:, :rows]
    return shifted + product_nt(query_u, key) + mask_row


def attend_kernel(
    own_ref, q_ref, k_ref, v_ref, rel_ref, bias_ref, mask_ref, out_ref, lse_ref, score_ref,
    *, slots, rows, tile
):
    own = own_ref[0]
    start = tile_start(own, pl.program_id(1), rows, tile)
    query_u, query_v = biased_queries(q_ref, bias_ref)
    top = jnp.full((tile, 1), -jnp.inf, f32)
    for s in range(slots):
        base = pl.multiple_of(slots * rows - tile - start + (own ^ s) * rows, tile)
        scores = slot_scores(
            query_u, query_v, k_ref[s], rel_ref[pl.ds(base, rows + tile), :],
            mask_ref[0:1, s * rows : (s + 1) * rows], rows, tile,
        )
        score_ref[s] = scores
        top = jnp.maximum(top, jnp.max(scores, axis=1, keepdims=True))
    total = jnp.zeros((tile, 1), f32)
    mixed = jnp.zeros((tile, HEAD_DIM), f32)
    for s in range(slots):
        weights = jnp.exp2(score_ref[s] - top)
        total = total + jnp.sum(weights, axis=1, keepdims=True)
        mixed = mixed + product(weights.astype(bf16), v_ref[s])
    out_ref[0] = (mixed / total).astype(bf16)
    lse_ref[0] = top + jnp.log2(total)


def attend_back_kernel(
    own_ref, q_ref, k_ref, v_ref, rel_ref, bias_ref, mask_ref, o_ref, do_ref, lse_ref,
    dq_ref, dk_ref, dv_ref, drel_ref, dbias_ref, dk_acc, dv_acc, *, slots, rows, tile
):
    own = own_ref[0]
    tile_at = pl.program_id(1)
    start = tile_start(own, tile_at, rows, tile)
    scale = HEAD_DIM**-0.5

    @pl.when(tile_at == 0)
    def _():
        dk_acc[...] = jnp.zeros_like(dk_acc)
        dv_acc[...] = jnp.zeros_like(dv_acc)
        drel_ref[...] = jnp.zeros_like(drel_ref)
        dbias_ref[...] = jnp.zeros_like(dbias_ref)

    query_u, query_v = biased_queries(q_ref, bias_ref)
    grad_out = do_ref[0]
    inner = jnp.sum(grad_out.astype(f32) * o_ref[0].astype(f32), axis=1, keepdims=True)
    lse = lse_ref[0]
    width = rows + tile
    row_at = lax.broadcasted_iota(jnp.int32, (tile, tile), 0)
    col_at = lax.broadcasted_iota(jnp.int32, (tile, tile), 1)
    flip = (row_at + col_at == tile - 1).astype(bf16)
    query_v_flip = product(flip, query_v).astype(bf16)
    grad_u = jnp.zeros((tile, HEAD_DIM), f32)
    grad_v_flip = jnp.zeros((tile, HEAD_DIM), f32)
    for s in range(slots):
        base = pl.multiple_of(slots * rows - tile - start + (own ^ s) * rows, tile)
        rel_window = rel_ref[pl.ds(base, width), :]
        key = k_ref[s]
        scores = slot_scores(
            query_u, query_v, key, rel_window, mask_ref[0:1, s * rows : (s + 1) * rows], rows, tile
        )
        probs = jnp.exp2(scores - lse)
        grad_probs = product_nt(grad_out, v_ref[s])
        grad_scores = (probs * (grad_probs - inner)).astype(bf16)
        dv_acc[s] += product_tn(probs.astype(bf16), grad_out)
        dk_acc[s] += product_tn(grad_scores, query_u)
        grad_u = grad_u + product(grad_scores, key)
        flipped = product(flip, grad_scores).astype(bf16)
        padded = jnp.concatenate([flipped, jnp.zeros((tile, width - rows), bf16)], axis=1)
        grad_raw = pltpu.roll(padded, 0, 1, stride=1, stride_axis=0)
        grad_v_flip = grad_v_flip + product(grad_raw, rel_window)
        drel_ref[pl.ds(base, width), :] += product_tn(grad_raw, query_v_flip)
    high = grad_v_flip.astype(bf16)
    low = (grad_v_flip - high.astype(f32)).astype(bf16)
    grad_v = product(flip, high) + product(flip, low)
    dbias_ref[0, 0:1, :] += jnp.sum(grad_u, axis=0, keepdims=True) * scale
    dbias_ref[0, 1:2, :] += jnp.sum(grad_v, axis=0, keepdims=True) * scale
    dq_ref[0] = ((grad_u + grad_v) * scale).astype(bf16)

    @pl.when(tile_at == pl.num_programs(1) - 1)
    def _():
        dk_ref[...] = (dk_acc[...] * (1.0 / LOG2E)).astype(bf16)
        dv_ref[...] = dv_acc[...].astype(bf16)
        drel_ref[...] = drel_ref[...] * (1.0 / LOG2E)


def attention_specs(slots, rows, heads, tile, first):
    per = rows // tile
    span = slots * rows
    by_tile = pl.BlockSpec((1, tile, HEAD_DIM), lambda h, i, own: (i // per, i % per, first + h))
    in_specs = [
        by_tile,
        pl.BlockSpec((slots, rows, HEAD_DIM), lambda h, i, own: (0, 0, heads + first + h)),
        pl.BlockSpec((slots, rows, HEAD_DIM), lambda h, i, own: (0, 0, 2 * heads + first + h)),
        pl.BlockSpec((2 * span, HEAD_DIM), lambda h, i, own: (0, first + h)),
        pl.BlockSpec((2, HEAD_DIM), lambda h, i, own: (0, first + h)),
        pl.BlockSpec((1, span), lambda h, i, own: (0, 0)),
    ]
    return slots * per, by_tile, in_specs


def attend(own, joint, rel, bias, mask, first, count, before=None):
    slots, rows, wide = joint.shape
    heads = wide // (3 * HEAD_DIM)
    span, tile = slots * rows, min(256, rows)
    tiles, by_tile, in_specs = attention_specs(slots, rows, heads, tile, first)
    by_row = pl.BlockSpec((1, tile, 1), lambda h, i, own: (first + h, i, 0))
    kernel = functools.partial(attend_kernel, slots=slots, rows=rows, tile=tile)
    operands, aliases = (own, joint, joint, joint, rel, bias, mask), {}
    if before is not None:
        operands += tuple(before)
        in_specs = in_specs + [pl.BlockSpec(memory_space=pl.ANY)] * 2
        aliases = {7: 0, 8: 1}

        def body_kernel(*refs):
            kernel(*refs[:7], *refs[9:])

    else:
        body_kernel = kernel
    return pl.pallas_call(
        body_kernel,
        grid_spec=pltpu.PrefetchScalarGridSpec(
            num_scalar_prefetch=1,
            grid=(count, tiles),
            in_specs=in_specs,
            out_specs=[by_tile, by_row],
            scratch_shapes=[pltpu.VMEM((slots, tile, rows), f32)],
        ),
        out_shape=[
            jax.ShapeDtypeStruct((slots, rows, heads * HEAD_DIM), bf16),
            jax.ShapeDtypeStruct((heads, span, 1), f32),
        ],
        input_output_aliases=aliases,
        compiler_params=pltpu.CompilerParams(vmem_limit_bytes=56 << 20),
        cost_estimate=pl.CostEstimate(
            flops=count * span * span * HEAD_DIM * 20,
            bytes_accessed=count * span * HEAD_DIM * 20,
            transcendentals=count * span * span,
        ),
        name="attend",
    )(*operands)


def attend_back(own, joint, rel, bias, mask, out, grad_out, lse):
    slots, rows, wide = joint.shape
    heads = wide // (3 * HEAD_DIM)
    span, tile = slots * rows, min(256, rows)
    tiles, by_tile, in_specs = attention_specs(slots, rows, heads, tile, 0)
    by_head = pl.BlockSpec((slots, rows, HEAD_DIM), lambda h, i, own: (0, 0, h))
    return pl.pallas_call(
        functools.partial(attend_back_kernel, slots=slots, rows=rows, tile=tile),
        grid_spec=pltpu.PrefetchScalarGridSpec(
            num_scalar_prefetch=1,
            grid=(heads, tiles),
            in_specs=in_specs
            + [by_tile, by_tile, pl.BlockSpec((1, tile, 1), lambda h, i, own: (h, i, 0))],
            out_specs=[
                by_tile,
                by_head,
                by_head,
                pl.BlockSpec((2 * span, HEAD_DIM), lambda h, i, own: (0, h)),
                pl.BlockSpec((1, 2, HEAD_DIM), lambda h, i, own: (h, 0, 0)),
            ],
            scratch_shapes=[pltpu.VMEM((slots, rows, HEAD_DIM), f32)] * 2,
        ),
        out_shape=[jax.ShapeDtypeStruct((slots, rows, heads * HEAD_DIM), bf16)] * 3
        + [
            jax.ShapeDtypeStruct((2 * span, heads * HEAD_DIM), f32),
            jax.ShapeDtypeStruct((heads, 2, HEAD_DIM), f32),
        ],
        compiler_params=pltpu.CompilerParams(vmem_limit_bytes=56 << 20),
        cost_estimate=pl.CostEstimate(
            flops=heads * span * span * HEAD_DIM * 50,
            bytes_accessed=heads * span * HEAD_DIM * 40,
            transcendentals=heads * span * span,
        ),
        name="attend_back",
    )(own, joint, joint, joint, rel, bias, mask, out, grad_out, lse)


def norm_fwd(values, gain_row, shift_row):
    centered = values - jnp.mean(values, axis=-1, keepdims=True)
    scale_inv = lax.rsqrt(jnp.mean(centered * centered, axis=-1, keepdims=True) + eps_norm)
    normal = centered * scale_inv
    return (normal * gain_row + shift_row, normal, scale_inv)


def norm_back(grad_out, normal, scale_inv, gain_row):
    grad_norm = grad_out * gain_row
    grad_in = scale_inv * (
        grad_norm
        - jnp.mean(grad_norm, axis=-1, keepdims=True)
        - normal * jnp.mean(grad_norm * normal, axis=-1, keepdims=True)
    )
    return (grad_in, jnp.sum(grad_out * normal, axis=0), jnp.sum(grad_out, axis=0))


def swish_grad(values):
    sigmoid_val = jax.nn.sigmoid(values)
    return sigmoid_val * (1.0 + values * (1.0 - sigmoid_val))


def sinusoid(distance, feat_width):
    half_width = feat_width // 2
    inv_freq = jnp.exp(jnp.arange(half_width, dtype=f32) * (-2.0 * math.log(10000.0) / feat_width))
    angles = distance[:, None] * inv_freq[None, :]
    return jnp.concatenate([jnp.sin(angles), jnp.cos(angles)], axis=1)


class Layout:
    def __init__(self, utt_count):
        self.dp, self.tm, self.utt = lax.axis_size("dp"), lax.axis_size("tm"), utt_count
        self.pairs = self.dp // 2
        self.size = self.tm // utt_count
        self.subs = self.size // 2
        dp_at, t = lax.axis_index("dp"), lax.axis_index("tm")
        self.core, self.t = dp_at % 2, t
        group, self.sub = t // self.subs, t % self.subs
        self.home_core, self.home_slot = group % 2, group // 2
        self.own = self.core * self.subs + self.sub

    def route(self, target):
        pairs = []
        for p in range(self.pairs):
            for c in range(2):
                for t in range(self.tm):
                    tp, tc, tt = target(p, c, t)
                    pairs.append(((2 * p + c) * self.tm + t, (2 * tp + tc) * self.tm + tt))
        return pairs

    def send(self, values, target):
        return lax.ppermute(values, AXES, self.route(target))

    def to_class(self, step):
        def target(p, c, t):
            other = (c * self.subs + t % self.subs) ^ step
            return p, other // self.subs, t - t % self.subs + other % self.subs

        return target

    def to_core(self, p, c, t):
        return p, 1 - c, t

    def home(self, step):
        def target(p, c, t):
            kind, at = t // self.utt, t % self.utt
            place = (step + at) % self.utt
            return p, kind // self.subs, (2 * place + c) * self.subs + kind % self.subs

        return target

    def enter(self, shard, step):
        at = (step + self.t % self.utt) % self.utt
        block = lax.dynamic_index_in_dim(shard, at, 0, keepdims=True)
        return self.send(block, self.home(step))

    def entered(self, blocks):
        result = jnp.zeros((self.utt,) + blocks[0].shape[1:], blocks[0].dtype)
        for k, block in enumerate(blocks):
            result = lax.dynamic_update_slice_in_dim(
                result, block, (self.home_slot - k) % self.utt, axis=0
            )
        return result

    def leave(self, blocks):
        received = []
        for k in range(self.utt):
            block = lax.dynamic_index_in_dim(
                blocks, (self.home_slot - k) % self.utt, 0, keepdims=True
            )
            there = self.route(self.home(k))
            received.append(lax.ppermute(block, AXES, [(b, a) for a, b in there]))
        return received

    def left(self, received):
        at = self.t % self.utt
        result = jnp.zeros((self.utt,) + received[0].shape[1:], received[0].dtype)
        for k, block in enumerate(received):
            result = lax.dynamic_update_slice_in_dim(result, block, (k + at) % self.utt, axis=0)
        return result

    def all_slots(self, values):
        parts = [values] + [self.send(values, self.to_class(s)) for s in range(1, self.size)]
        return jnp.concatenate(parts, axis=0)

    def own_sum(self, partial):
        parts = partial.reshape((self.size, -1) + partial.shape[1:])
        total = parts[0]
        for s in range(1, self.size):
            total = total + self.send(parts[s].astype(bf16), self.to_class(s)).astype(f32)
        return total

    def over_utterances(self, values, join):
        step = 1
        groups = 2 * self.utt
        while step < self.pairs * groups:

            def target(p, c, t, step=step):
                other = (p * groups + t // self.subs) ^ step
                return other // groups, c, (other % groups) * self.subs + t % self.subs

            values = join(values, self.send(values, target))
            step *= 2
        return values

    def core_half(self, values, axis):
        shape = values.shape
        split = values.reshape(shape[:axis] + (2, shape[axis] // 2) + shape[axis + 1 :])
        return lax.dynamic_index_in_dim(split, self.core, axis, keepdims=False)

    def sub_part(self, values, axis):
        if self.subs == 1:
            return values
        width = values.shape[axis] // self.subs
        return lax.dynamic_slice_in_dim(values, self.sub * width, width, axis)

    def sub_place(self, values, axis):
        if self.subs == 1:
            return values
        width = values.shape[axis]
        shape = list(values.shape)
        shape[axis] = width * self.subs
        return lax.dynamic_update_slice_in_dim(
            jnp.zeros(shape, values.dtype), values, self.sub * width, axis
        )

    def cols_half(self, local, groups):
        rows, cols = local.shape
        split = local.reshape(rows, groups, 2, cols // (2 * groups))
        return lax.dynamic_index_in_dim(split, self.core, 2, keepdims=False).reshape(rows, cols // 2)

    def cols_join(self, halves, groups):
        _, rows, cols = halves.shape
        split = halves.reshape(2, rows, groups, cols // groups)
        return split.transpose(1, 2, 0, 3).reshape(rows, 2 * cols)

    def gather_small(self, local):
        parts = local[None]
        step = 1
        while step < self.tm:
            parts = jnp.concatenate(
                [parts, self.send(parts, lambda p, c, t, step=step: (p, c, t ^ step))], axis=0
            )
            step *= 2
        parts = jnp.take(parts, jnp.arange(self.tm, dtype=jnp.int32) ^ self.t, axis=0)
        return parts.transpose(1, 0, 2).reshape(local.shape[0], -1)

    def sum_all(self, values):
        step = 1
        while step < self.size:
            values = values + self.send(values, self.to_class(step))
            step *= 2
        return self.over_utterances(values, jnp.add)

    def gather(self, locals_, ready=None):
        plane = lax.axis_index("dp") // 2
        parts = [lax.dynamic_slice_in_dim(v, plane * (v.shape[0] // self.pairs), v.shape[0] // self.pairs, 0) for v in locals_]
        packed, places = pack(parts)
        if ready is not None:
            ready.append(packed)
        groups = [
            [(2 * p + c) * self.tm + t for t in range(self.tm) for p in range(self.pairs)]
            for c in range(2)
        ]
        full = lax.all_gather(packed[None], AXES, axis=0, tiled=True, axis_index_groups=groups)
        return [v.reshape(-1, v.shape[-1]) for v in unpack(full, places)]

    def scatter(self, grads, over_planes=False, after=None):
        plane = lax.axis_index("dp") // 2
        split = [g.astype(bf16).reshape(self.tm, self.pairs, -1, g.shape[-1]) for g in grads]

        def part(at):
            return pack([lax.dynamic_index_in_dim(v, at, 1, keepdims=False) for v in split])

        mine, places = part(plane)
        if over_planes:
            for s in range(1, self.pairs):
                other = self.send(part(plane ^ s)[0], lambda p, c, t, s=s: (p ^ s, c, t))
                mine = (mine.astype(f32) + other.astype(f32)).astype(bf16)
        else:
            mine = jnp.stack([part(plane ^ s)[0] for s in range(self.pairs)], axis=1)
        if after is not None:
            mine, _ = lax.optimization_barrier((mine, after))
        return lax.psum_scatter(mine, "tm", scatter_dimension=0, tiled=True), places

    def collect(self, mine, places):
        plane = lax.axis_index("dp") // 2
        if mine.ndim == 4:
            parts = mine
            mine = parts[:, 0].astype(f32)
            for s in range(1, self.pairs):
                mine = mine + self.send(parts[:, s], lambda p, c, t, s=s: (p ^ s, c, t)).astype(f32)
            mine = mine.astype(bf16)
        whole = jnp.zeros((self.pairs,) + mine.shape[1:], bf16)
        whole = lax.dynamic_update_slice_in_dim(whole, mine, plane, 0)
        for s in range(1, self.pairs):
            other = self.send(mine, lambda p, c, t, s=s: (p ^ s, c, t))
            whole = lax.dynamic_update_slice_in_dim(whole, other, plane ^ s, 0)
        there = self.send(whole, self.to_core)
        both = jnp.stack(
            [jnp.where(self.core == 0, whole, there), jnp.where(self.core == 0, there, whole)]
        )
        return [v.astype(f32).reshape(2, -1, v.shape[-1]) for v in unpack(both, places)]


def pack(parts):
    blocks, places, row, spare = [], [], 0, None
    for v in parts:
        rows, cols, own = v.shape[-2], v.shape[-1], []
        for at in range(0, cols - D + 1, D):
            blocks.append([v[..., at : at + D]])
            own.append((row, 0, rows, D))
            row += rows
        if cols % D:
            piece = v[..., cols - cols % D :]
            if spare is not None and spare[1] == rows and spare[2] + cols % D <= D:
                blocks[spare[0]].append(piece)
                own.append((spare[3], spare[2], rows, cols % D))
                spare = None
            else:
                spare = (len(blocks), rows, cols % D, row)
                blocks.append([piece])
                own.append((row, 0, rows, cols % D))
                row += rows
        places.append(own)
    filled = []
    for block in blocks:
        joined = block[0] if len(block) == 1 else jnp.concatenate(block, axis=-1)
        if joined.shape[-1] < D:
            pads = [(0, 0)] * (joined.ndim - 1) + [(0, D - joined.shape[-1])]
            joined = jnp.pad(joined, pads)
        filled.append(joined)
    return jnp.concatenate(filled, axis=-2), places


def unpack(packed, places):
    results = []
    for own in places:
        pieces = [packed[..., r : r + n, c : c + m] for r, c, n, m in own]
        results.append(pieces[0] if len(pieces) == 1 else jnp.concatenate(pieces, axis=-1))
    return results


def merge_moments(left, right):
    count_a, mean_a, square_a = left[0], left[1], left[2]
    count_b, mean_b, square_b = right[0], right[1], right[2]
    count = count_a + count_b
    gap = mean_a - mean_b
    mean = (count_a * mean_a + count_b * mean_b) / count
    square = (square_a + square_b) + gap * gap * (count_a * count_b / count)
    return jnp.stack([count, mean, square])


def body(
    inputs,
    cotangent,
    lengths,
    first_up,
    first_down,
    joint_proj,
    rel_proj,
    merge_proj,
    conv_wide,
    conv_narrow,
    second_up,
    second_down,
    norm_gains,
    norm_shifts,
    pos_biases,
    depth_taps,
):
    lay = Layout(inputs.shape[0])
    utt_count, block_len, _ = inputs.shape
    tm, size, own = lay.tm, lay.size, lay.own
    rows = utt_count * block_len
    span = rows * size
    feats = D // size
    pad_width = KW // 2

    def own_feats(values):
        count = values.shape[0]
        split = values.reshape(count, tm, 2, D // (2 * tm))
        half = lax.dynamic_index_in_dim(split, lay.core, 2, keepdims=False)
        return lay.sub_part(half.reshape(count, D // 2), 1)

    def place_feats(values):
        count = values.shape[0]
        half = lay.sub_place(values, 1).reshape(count, tm, 1, D // (2 * tm))
        pick = (jnp.arange(2) == lay.core).astype(f32)[None, None, :, None]
        return (half * pick).reshape(count, D)

    def place_heads(values):
        return lax.dynamic_update_slice_in_dim(
            jnp.zeros((values.shape[0], D), f32), values, own * feats, axis=1
        )

    ready = []
    up_one, down_one, joint_half, rel_half = lay.gather(
        [
            lay.cols_half(first_up, tm),
            lay.core_half(first_down, 0),
            lay.cols_half(joint_proj, 3),
            lay.cols_half(rel_proj, 1),
        ],
        ready,
    )
    _, inputs, norm_gains = lax.optimization_barrier((ready[0], inputs, norm_gains))
    small = jnp.concatenate([norm_gains, norm_shifts, pos_biases, depth_taps], axis=0)
    small = lay.gather_small(small).astype(f32)
    gain_rows, shift_rows = small[0:6], small[6:12]

    bias_rows = lax.dynamic_slice_in_dim(small[12:14], own * feats, feats, axis=1)
    kernel_taps = own_feats(small[14 : 14 + KW])
    batch_gain, batch_shift = own_feats(gain_rows[5:6])[0], own_feats(shift_rows[5:6])[0]

    merge_full, wide_half, narrow_half, up_two, down_two = lay.gather(
        [
            merge_proj,
            lay.cols_half(conv_wide, 2 * tm),
            lay.core_half(conv_narrow, 0),
            lay.cols_half(second_up, tm),
            lay.core_half(second_down, 0),
        ]
    )
    up_one, down_one = lay.sub_part(up_one, 1), lay.sub_part(down_one, 0)
    up_two, down_two = lay.sub_part(up_two, 1), lay.sub_part(down_two, 0)
    joint_own = lay.sub_part(joint_half.reshape(D, 3, D // 2), 2).reshape(D, 3 * feats)
    rel_own = lay.sub_part(rel_half, 1)
    wide_own = lay.sub_part(wide_half.reshape(D, 2, D // 2), 2).reshape(D, 2 * feats)
    narrow_own = lay.sub_part(narrow_half, 0)
    def feed_forward(values, gain_row, shift_row, up_weight, down_weight):
        normed, normal, scale_inv = norm_fwd(values, gain_row, shift_row)
        normed_low = lay.all_slots(normed.astype(bf16))
        hidden = product(normed_low, up_weight)
        active_low = (hidden * jax.nn.sigmoid(hidden)).astype(bf16)
        result = lay.own_sum(product(active_low, down_weight))
        return (result, (normal, scale_inv, normed_low, hidden, active_low))

    def feed_back(grad_result, saved_acts, gain_row, up_weight, down_weight, between):
        normal, scale_inv, normed_low, hidden, active_low = saved_acts
        grad_low = lay.all_slots(grad_result.astype(bf16))
        grad_down = product_tn(active_low, grad_low).astype(bf16)
        grad_down, grad_low = lax.optimization_barrier((grad_down, grad_low))
        grad_hidden = (product_nt(grad_low, down_weight) * swish_grad(hidden)).astype(bf16)
        grad_up = product_tn(normed_low, grad_hidden).astype(bf16)
        grad_down, grad_up = lay.sub_place(grad_down, 0), lay.sub_place(grad_up, 1)
        grad_hidden, moved = between(grad_down, grad_up, grad_hidden)
        grad_values, grad_gain, grad_shift = norm_back(
            lay.own_sum(product_nt(grad_hidden, up_weight)), normal, scale_inv, gain_row
        )
        return (grad_values, moved, grad_gain, grad_shift)

    group_lengths = jnp.where(
        lay.home_core == lay.core, lengths, lay.send(lengths, lay.to_core)
    )
    length = lax.dynamic_index_in_dim(group_lengths, lay.home_slot, 0, keepdims=False)
    slot_class = jnp.arange(size, dtype=jnp.int32) ^ own
    frame_pos = slot_class[:, None] * rows + jnp.arange(rows, dtype=jnp.int32)[None, :]
    live = frame_pos < length
    live_col = live.astype(f32)[:, :, None]
    key_mask = jnp.where(live, 0.0, neg_fill).astype(f32).reshape(1, span)
    own_at = own.reshape(1).astype(jnp.int32)

    def framed_rows(values):
        last, leading = values[:, rows - pad_width :], values[:, :pad_width]
        before, after = [], []
        for s in range(size):
            kind = own ^ s
            prev = lax.dynamic_index_in_dim(last, jnp.maximum(kind - 1, 0) ^ own, 0)
            following = lax.dynamic_index_in_dim(
                leading, jnp.minimum(kind + 1, size - 1) ^ own, 0
            )
            before.append(jnp.where(kind > 0, prev, 0.0))
            after.append(jnp.where(kind < size - 1, following, 0.0))
        return jnp.concatenate(
            [jnp.concatenate(before, axis=0), values, jnp.concatenate(after, axis=0)], axis=1
        )

    distance = (span - 1 - jnp.arange(2 * span, dtype=jnp.int32)).astype(f32)
    table_low = sinusoid(distance, D).astype(bf16)
    up_one, table_low = lax.optimization_barrier((up_one, table_low))
    steps = range(utt_count)
    section_zero = lay.entered([lay.enter(inputs, k) for k in steps]).astype(f32).reshape(rows, D)
    branch_one, saved_one = feed_forward(
        section_zero, gain_rows[0], shift_rows[0], up_one, down_one
    )
    section_one = section_zero + 0.5 * branch_one
    att_normed, att_normal, att_inv = norm_fwd(section_one, gain_rows[1], shift_rows[1])
    att_low = lay.all_slots(att_normed.astype(bf16))
    joint_out = product(att_low, joint_own).astype(bf16).reshape(size, rows, 3 * feats)
    rel_low = product(table_low, rel_own).astype(bf16)
    heads = feats // HEAD_DIM
    attended, log_totals = attend(own_at, joint_out, rel_low, bias_rows, key_mask, 0, heads)

    merge_full, cotangent = lax.optimization_barrier((merge_full, cotangent))
    entries = [lay.enter(cotangent, k) for k in steps]
    merge_slots = jnp.concatenate(
        [
            lax.dynamic_slice_in_dim(merge_full, (own ^ s) * feats, feats, axis=0)
            for s in range(size)
        ],
        axis=0,
    )
    attended_low = jnp.concatenate(
        [attended[0]] + [lay.send(attended[s], lay.to_class(s)) for s in range(1, size)], axis=1
    )
    section_two = section_one + product(attended_low, merge_slots)
    conv_normed, conv_normal, conv_inv = norm_fwd(section_two, gain_rows[2], shift_rows[2])
    conv_low = lay.all_slots(conv_normed.astype(bf16))
    wide_out = product(conv_low, wide_own).reshape(size, rows, 2 * feats)
    lin_half = wide_out[:, :, :feats]
    gate_sig = jax.nn.sigmoid(wide_out[:, :, feats:])
    gated = lin_half * gate_sig * live_col
    framed = framed_rows(gated)
    depth_out = kernel_taps[0] * framed[:, 0:rows]
    for offset in range(1, KW):
        depth_out = depth_out + kernel_taps[offset] * framed[:, offset : offset + rows]
    own_count = length.astype(f32)
    own_mean = jnp.sum(depth_out * live_col, axis=(0, 1)) / own_count
    own_gap = (depth_out - own_mean) * live_col
    moments = jnp.stack(
        [jnp.broadcast_to(own_count, (feats,)), own_mean, jnp.sum(own_gap * own_gap, axis=(0, 1))]
    )
    moments, entries = lax.optimization_barrier((moments, entries))
    total_count, bn_mean, total_var = lay.over_utterances(moments, merge_moments)
    bn_inv = lax.rsqrt(total_var / total_count + eps_norm)
    bn_normal = (depth_out - bn_mean) * bn_inv
    bn_flat = bn_normal * batch_gain + batch_shift
    swish_low = (bn_flat * jax.nn.sigmoid(bn_flat)).astype(bf16).reshape(span, feats)
    section_three = section_two + lay.own_sum(product(swish_low, narrow_own))
    branch_four, saved_four = feed_forward(
        section_three, gain_rows[3], shift_rows[3], up_two, down_two
    )
    section_four = section_three + 0.5 * branch_four
    final_out, final_normal, final_inv = norm_fwd(section_four, gain_rows[4], shift_rows[4])
    final_low = final_out.astype(bf16).reshape(utt_count, block_len, D)

    grad_final = lay.entered(entries).astype(f32).reshape(rows, D)
    grad_four, gain_four, shift_four = norm_back(grad_final, final_normal, final_inv, gain_rows[4])

    def scatter_two(grad_down, grad_up, grad_hidden):
        grad_up, grad_hidden = lax.optimization_barrier((grad_up, grad_hidden))
        return grad_hidden, (lay.scatter([grad_up]), lay.scatter([grad_down]))

    grad_mid, (moved_up_two, moved_down_two), gain_three, shift_three = feed_back(
        0.5 * grad_four, saved_four, gain_rows[3], up_two, down_two, scatter_two
    )
    grad_three = grad_four + grad_mid
    narrow_low = lay.all_slots(grad_three.astype(bf16))
    grad_narrow = lay.sub_place(product_tn(swish_low, narrow_low), 0)
    grad_batch = product_nt(narrow_low, narrow_own).reshape(size, rows, feats) * swish_grad(bn_flat)
    gain_batch = jnp.sum(grad_batch * bn_normal, axis=(0, 1))
    shift_batch = jnp.sum(grad_batch, axis=(0, 1))
    grad_hat = grad_batch * batch_gain
    total_hat, total_cross = lay.over_utterances(
        jnp.stack([shift_batch * batch_gain, gain_batch * batch_gain]), jnp.add
    )
    grad_depth = bn_inv * (
        grad_hat - live_col / total_count * (total_hat + bn_normal * total_cross)
    )
    grad_framed = framed_rows(grad_depth)
    grad_gated = kernel_taps[0] * grad_framed[:, KW - 1 : KW - 1 + rows]
    for offset in range(1, KW):
        grad_gated = (
            grad_gated + kernel_taps[offset] * grad_framed[:, KW - 1 - offset : KW - 1 - offset + rows]
        )
    grad_taps = jnp.stack(
        [
            jnp.sum(grad_depth * framed[:, offset : offset + rows], axis=(0, 1))
            for offset in range(KW)
        ]
    )
    grad_glu = grad_gated * live_col
    grad_wide_out = (
        jnp.concatenate(
            [grad_glu * gate_sig, grad_glu * lin_half * gate_sig * (1.0 - gate_sig)], axis=2
        )
        .astype(bf16)
        .reshape(span, 2 * feats)
    )
    grad_wide = lay.sub_place(product_tn(conv_low, grad_wide_out).reshape(D, 2, feats), 2)
    grad_conv_in, gain_two, shift_two = norm_back(
        lay.own_sum(product_nt(grad_wide_out, wide_own)), conv_normal, conv_inv, gain_rows[2]
    )
    grad_two = grad_three + grad_conv_in
    merge_low = grad_two.astype(bf16)
    grad_merge = product_tn(attended_low, merge_low).astype(bf16)
    grad_merge = jnp.concatenate(
        [
            lax.dynamic_slice_in_dim(grad_merge, (own ^ s) * feats, feats, axis=0)
            for s in range(size)
        ],
        axis=0,
    )
    halves = grad_merge.reshape(D, 2, D // 2)
    mine = lax.dynamic_index_in_dim(halves, lay.core, 1, keepdims=False)
    theirs = lax.dynamic_index_in_dim(halves, 1 - lay.core, 1, keepdims=False)
    grad_merge = mine.astype(f32) + lay.send(theirs, lay.to_core).astype(f32)
    grad_attended = product_nt(merge_low, merge_slots).astype(bf16).reshape(rows, size, feats)
    grad_attended = jnp.stack(
        [grad_attended[:, 0]]
        + [lay.send(grad_attended[:, s], lay.to_class(s)) for s in range(1, size)]
    )
    grad_attended, final_low = lax.optimization_barrier((grad_attended, final_low))
    output = lay.leave(final_low)
    moved_conv = lay.scatter([grad_merge, grad_wide.reshape(D, D), grad_narrow])
    grad_query, grad_key, grad_value, grad_rel, grad_biases = attend_back(
        own_at, joint_out, rel_low, bias_rows, key_mask, attended, grad_attended, log_totals
    )
    grad_query, rows_up_two, rows_down_two, rows_conv, output = lax.optimization_barrier(
        (grad_query, moved_up_two[0], moved_down_two[0], moved_conv[0], output)
    )
    grad_biases = grad_biases.transpose(1, 0, 2).reshape(2, feats)
    rel_high = grad_rel.astype(bf16)
    rel_rest = (grad_rel - rel_high.astype(f32)).astype(bf16)
    grad_rel_proj = lay.sub_place(
        product_tn(table_low, rel_high) + product_tn(table_low, rel_rest), 1
    )
    grad_joint_out = jnp.concatenate([grad_query, grad_key, grad_value], axis=2).reshape(
        span, 3 * feats
    )
    grad_joint = lay.sub_place(product_tn(att_low, grad_joint_out).reshape(D, 3, feats), 2)
    grad_att_in, gain_one, shift_one = norm_back(
        lay.own_sum(product_nt(grad_joint_out, joint_own)), att_normal, att_inv, gain_rows[1]
    )
    grad_one = grad_two + grad_att_in
    earlier = (rows_up_two, rows_down_two, rows_conv, output)
    moved_joint = lay.scatter(
        [grad_joint.reshape(D, 3 * D // 2), grad_rel_proj], after=rows_conv
    )

    def scatter_one(grad_down, grad_up, grad_hidden):
        grad_hidden, rows_joint = lax.optimization_barrier((grad_hidden, moved_joint[0]))
        moved_down = lay.scatter([grad_down], after=rows_joint)
        moved_up = lay.scatter([grad_up], over_planes=True, after=moved_down[0])
        late, _ = lax.optimization_barrier((earlier + (rows_joint,), grad_up))
        return grad_hidden, (moved_down, moved_up, late)

    grad_first, (moved_down, moved_up, late), gain_zero, shift_zero = feed_back(
        0.5 * grad_one, saved_one, gain_rows[0], up_one, down_one, scatter_one
    )
    grad_zero = grad_one + grad_first
    grad_inputs = lay.left(lay.leave(grad_zero.astype(bf16).reshape(utt_count, block_len, D)))

    rows_up_two, rows_down_two, rows_conv, output, rows_joint = late
    output = lay.left(output)
    (summed_up_two,) = lay.collect(rows_up_two, moved_up_two[1])
    (summed_down_two,) = lay.collect(rows_down_two, moved_down_two[1])
    summed_merge, summed_wide, summed_narrow = lay.collect(rows_conv, moved_conv[1])
    summed_joint, summed_rel = lay.collect(rows_joint, moved_joint[1])
    (summed_down_one,) = lay.collect(*moved_down)
    (summed_up_one,) = lay.collect(*moved_up)
    summed_up_one = lay.cols_join(summed_up_one, tm)
    summed_up_two = lay.cols_join(summed_up_two, tm)
    summed_joint = lay.cols_join(summed_joint, 3)
    summed_rel = lay.cols_join(summed_rel, 1)
    summed_merge = lay.cols_join(summed_merge, 1)
    summed_wide = lay.cols_join(summed_wide, 2 * tm)
    summed_down_one = summed_down_one.reshape(-1, D)
    summed_down_two = summed_down_two.reshape(-1, D)
    summed_narrow = summed_narrow.reshape(-1, D)

    small_grads = jnp.concatenate(
        [
            jnp.stack([gain_zero, gain_one, gain_two, gain_three, gain_four]),
            place_feats(gain_batch[None]),
            jnp.stack([shift_zero, shift_one, shift_two, shift_three, shift_four]),
            place_feats(shift_batch[None]),
            place_heads(grad_biases),
            place_feats(grad_taps),
        ],
        axis=0,
    )
    small_grads = lay.sum_all(small_grads)
    small_grads = lax.dynamic_slice_in_dim(small_grads, lay.t * (D // tm), D // tm, axis=1)
    return (
        output,
        grad_inputs,
        summed_up_one,
        summed_down_one,
        summed_joint,
        summed_rel,
        summed_merge,
        summed_wide,
        summed_narrow,
        summed_up_two,
        summed_down_two,
        small_grads[0:6],
        small_grads[6:12],
        small_grads[12:14],
        small_grads[14 : 14 + KW],
    )


def solution(mesh):
    frames = P("dp", "tm", None)
    rows, cols = P("tm", None), P(None, "tm")
    return jax.shard_map(
        body,
        mesh=mesh,
        in_specs=(frames, frames, P("dp")) + (rows,) * 9 + (cols,) * 4,
        out_specs=(frames, frames) + (rows,) * 9 + (cols,) * 4,
        check_vma=False,
    )
```

```python
import functools
import math

import jax
import jax.numpy as jnp
from jax import lax
from jax.experimental import pallas as pl
from jax.experimental.pallas import tpu as pltpu
from jax.sharding import PartitionSpec as P

D = 1024
HEADS = 8
HEAD_DIM = 128
KW = 5

AXES = ("dp", "tm")
LOG2E = math.log2(math.e)
eps_norm = 1e-05
neg_fill = -1e30
f32 = jnp.float32
bf16 = jnp.bfloat16


def product(left, right):
    return jnp.dot(left, right, preferred_element_type=f32)


def product_nt(left, right):
    return lax.dot_general(left, right, (((1,), (1,)), ((), ())), preferred_element_type=f32)


def product_tn(left, right):
    return lax.dot_general(left, right, (((0,), (0,)), ((), ())), preferred_element_type=f32)


def tile_start(own, tile_at, rows, tile):
    per = rows // tile
    return ((tile_at // per) ^ own) * rows + (tile_at % per) * tile


def biased_queries(q_ref, bias_ref):
    query = q_ref[0].astype(f32)
    scale = HEAD_DIM**-0.5 * LOG2E
    query_u = ((query + bias_ref[0:1, :]) * scale).astype(bf16)
    query_v = ((query + bias_ref[1:2, :]) * scale).astype(bf16)
    return query_u, query_v


def shifted_rel(query_v, rel_window, rows, tile):
    width = rows + tile
    raw = product_nt(query_v, rel_window)
    return pltpu.roll(raw, width - (tile - 1), 1, stride=1, stride_axis=0)[:, :rows]


def three_parts(column):
    high = column.astype(bf16).astype(f32)
    middle = (column - high).astype(bf16).astype(f32)
    return high, middle, column - high - middle


def widened(values, mask_factor, column=None):
    lane = lax.broadcasted_iota(jnp.int32, (values.shape[0], HEAD_DIM), 1)
    extra = jnp.where(lane == 0, mask_factor, 0.0)
    if column is not None:
        for at, part in enumerate(three_parts(column)):
            extra = jnp.where(lane == at + 1, part, extra)
    return jnp.concatenate([values, extra.astype(bf16)], axis=1)


def fill_wide(wide_ref, ref, extra_ref):
    wide_ref[:, :, :HEAD_DIM] = ref[...]
    wide_ref[:, :, HEAD_DIM:] = extra_ref[...]


def attend_kernel(
    own_ref, q_ref, k_ref, v_ref, rel_ref, bias_ref, mask_ref, out_ref, lse_ref, score_ref,
    *, slots, rows, tile
):
    own = own_ref[0]
    start = tile_start(own, pl.program_id(1), rows, tile)
    query_u, query_v = biased_queries(q_ref, bias_ref)
    top = jnp.full((tile, 1), -jnp.inf, f32)
    for s in range(slots):
        base = pl.multiple_of(slots * rows - tile - start + (own ^ s) * rows, tile)
        scores = shifted_rel(query_v, rel_ref[pl.ds(base, rows + tile), :], rows, tile)
        scores = scores + product_nt(query_u, k_ref[s])
        scores = scores + mask_ref[0:1, s * rows : (s + 1) * rows]
        score_ref[s] = scores
        top = jnp.maximum(top, jnp.max(scores, axis=1, keepdims=True))
    total = jnp.zeros((tile, 1), f32)
    mixed = jnp.zeros((tile, HEAD_DIM), f32)
    for s in range(slots):
        weights = jnp.exp2(score_ref[s] - top)
        total = total + jnp.sum(weights, axis=1, keepdims=True)
        mixed = mixed + product(weights.astype(bf16), v_ref[s])
    out_ref[0] = (mixed / total).astype(bf16)
    lse_ref[0] = top + jnp.log2(total)


def attend_back_kernel(
    own_ref, q_ref, k_ref, v_ref, rel_ref, bias_ref, extra_ref, o_ref, do_ref, lse_ref,
    dq_ref, dk_ref, dv_ref, drel_ref, dbias_ref, dk_acc, dv_acc, key_ref, value_ref,
    *, slots, rows, tile
):
    own = own_ref[0]
    tile_at = pl.program_id(1)
    start = tile_start(own, tile_at, rows, tile)
    scale = HEAD_DIM**-0.5

    @pl.when(tile_at == 0)
    def _():
        fill_wide(key_ref, k_ref, extra_ref)
        fill_wide(value_ref, v_ref, extra_ref)
        dk_acc[...] = jnp.zeros_like(dk_acc)
        dv_acc[...] = jnp.zeros_like(dv_acc)
        drel_ref[...] = jnp.zeros_like(drel_ref)
        dbias_ref[...] = jnp.zeros_like(dbias_ref)

    query_u, query_v = biased_queries(q_ref, bias_ref)
    grad_out = do_ref[0]
    inner = jnp.sum(grad_out.astype(f32) * o_ref[0].astype(f32), axis=1, keepdims=True)
    query_wide = widened(query_u, 1.0, -lse_ref[0])
    grad_wide = widened(grad_out, 0.0, -inner)
    width = rows + tile
    row_at = lax.broadcasted_iota(jnp.int32, (tile, tile), 0)
    col_at = lax.broadcasted_iota(jnp.int32, (tile, tile), 1)
    flip = (row_at + col_at == tile - 1).astype(bf16)
    query_v_flip = product(flip, query_v).astype(bf16)
    grad_u = jnp.zeros((tile, HEAD_DIM), f32)
    grad_v_flip = jnp.zeros((tile, HEAD_DIM), f32)
    for s in range(slots):
        base = pl.multiple_of(slots * rows - tile - start + (own ^ s) * rows, tile)
        rel_window = rel_ref[pl.ds(base, width), :]
        scores = shifted_rel(query_v, rel_window, rows, tile)
        probs = jnp.exp2(scores + product_nt(query_wide, key_ref[s]))
        grad_scores = (probs * product_nt(grad_wide, value_ref[s])).astype(bf16)
        dv_acc[s] += product_tn(probs.astype(bf16), grad_out)
        dk_acc[s] += product_tn(grad_scores, query_u)
        grad_u = grad_u + product(grad_scores, k_ref[s])
        flipped = product(flip, grad_scores).astype(bf16)
        padded = jnp.concatenate([flipped, jnp.zeros((tile, width - rows), bf16)], axis=1)
        grad_raw = pltpu.roll(padded, 0, 1, stride=1, stride_axis=0)
        grad_v_flip = grad_v_flip + product(grad_raw, rel_window)
        drel_ref[pl.ds(base, width), :] += product_tn(grad_raw, query_v_flip)
    high = grad_v_flip.astype(bf16)
    low = (grad_v_flip - high.astype(f32)).astype(bf16)
    grad_v = product(flip, high) + product(flip, low)
    dbias_ref[0, 0:1, :] += jnp.sum(grad_u, axis=0, keepdims=True) * scale
    dbias_ref[0, 1:2, :] += jnp.sum(grad_v, axis=0, keepdims=True) * scale
    dq_ref[0] = ((grad_u + grad_v) * scale).astype(bf16)

    @pl.when(tile_at == pl.num_programs(1) - 1)
    def _():
        dk_ref[...] = (dk_acc[...] * (1.0 / LOG2E)).astype(bf16)
        dv_ref[...] = dv_acc[...].astype(bf16)
        drel_ref[...] = drel_ref[...] * (1.0 / LOG2E)


def attention_specs(slots, rows, heads, tile):
    per = rows // tile
    span = slots * rows
    by_tile = pl.BlockSpec((1, tile, HEAD_DIM), lambda h, i, own: (i // per, i % per, h))
    in_specs = [
        by_tile,
        pl.BlockSpec((slots, rows, HEAD_DIM), lambda h, i, own: (0, 0, heads + h)),
        pl.BlockSpec((slots, rows, HEAD_DIM), lambda h, i, own: (0, 0, 2 * heads + h)),
        pl.BlockSpec((2 * span, HEAD_DIM), lambda h, i, own: (0, h)),
        pl.BlockSpec((2, HEAD_DIM), lambda h, i, own: (0, h)),
        pl.BlockSpec((slots, rows, HEAD_DIM), lambda h, i, own: (0, 0, 0)),
    ]
    return slots * per, by_tile, in_specs


def attend(own, joint, rel, bias, mask):
    slots, rows, wide = joint.shape
    heads = wide // (3 * HEAD_DIM)
    span, tile = slots * rows, min(256, rows)
    tiles, by_tile, in_specs = attention_specs(slots, rows, heads, tile)
    return pl.pallas_call(
        functools.partial(attend_kernel, slots=slots, rows=rows, tile=tile),
        grid_spec=pltpu.PrefetchScalarGridSpec(
            num_scalar_prefetch=1,
            grid=(heads, tiles),
            in_specs=in_specs[:-1] + [pl.BlockSpec((1, span), lambda h, i, own: (0, 0))],
            out_specs=[by_tile, pl.BlockSpec((1, tile, 1), lambda h, i, own: (h, i, 0))],
            scratch_shapes=[pltpu.VMEM((slots, tile, rows), f32)],
        ),
        out_shape=[
            jax.ShapeDtypeStruct((slots, rows, heads * HEAD_DIM), bf16),
            jax.ShapeDtypeStruct((heads, span, 1), f32),
        ],
        compiler_params=pltpu.CompilerParams(vmem_limit_bytes=56 << 20),
        cost_estimate=pl.CostEstimate(
            flops=heads * span * span * HEAD_DIM * 20,
            bytes_accessed=heads * span * HEAD_DIM * 20,
            transcendentals=heads * span * span,
        ),
        name="attend",
    )(own, joint, joint, joint, rel, bias, mask)


def attend_back(own, joint, rel, bias, extra, out, grad_out, lse):
    slots, rows, wide = joint.shape
    heads = wide // (3 * HEAD_DIM)
    span, tile = slots * rows, min(256, rows)
    tiles, by_tile, in_specs = attention_specs(slots, rows, heads, tile)
    by_head = pl.BlockSpec((slots, rows, HEAD_DIM), lambda h, i, own: (0, 0, h))
    return pl.pallas_call(
        functools.partial(attend_back_kernel, slots=slots, rows=rows, tile=tile),
        grid_spec=pltpu.PrefetchScalarGridSpec(
            num_scalar_prefetch=1,
            grid=(heads, tiles),
            in_specs=in_specs
            + [by_tile, by_tile, pl.BlockSpec((1, tile, 1), lambda h, i, own: (h, i, 0))],
            out_specs=[
                by_tile,
                by_head,
                by_head,
                pl.BlockSpec((2 * span, HEAD_DIM), lambda h, i, own: (0, h)),
                pl.BlockSpec((1, 2, HEAD_DIM), lambda h, i, own: (h, 0, 0)),
            ],
            scratch_shapes=[pltpu.VMEM((slots, rows, HEAD_DIM), f32)] * 2
            + [pltpu.VMEM((slots, rows, 2 * HEAD_DIM), bf16)] * 2,
        ),
        out_shape=[jax.ShapeDtypeStruct((slots, rows, heads * HEAD_DIM), bf16)] * 3
        + [
            jax.ShapeDtypeStruct((2 * span, heads * HEAD_DIM), f32),
            jax.ShapeDtypeStruct((heads, 2, HEAD_DIM), f32),
        ],
        compiler_params=pltpu.CompilerParams(vmem_limit_bytes=56 << 20),
        cost_estimate=pl.CostEstimate(
            flops=heads * span * span * HEAD_DIM * 50,
            bytes_accessed=heads * span * HEAD_DIM * 40,
            transcendentals=heads * span * span,
        ),
        name="attend_back",
    )(own, joint, joint, joint, rel, bias, extra, out, grad_out, lse)


def norm_fwd(values, gain_row, shift_row):
    centered = values - jnp.mean(values, axis=-1, keepdims=True)
    scale_inv = lax.rsqrt(jnp.mean(centered * centered, axis=-1, keepdims=True) + eps_norm)
    normal = centered * scale_inv
    return (normal * gain_row + shift_row, normal, scale_inv)


def norm_back(grad_out, normal, scale_inv, gain_row):
    grad_norm = grad_out * gain_row
    grad_in = scale_inv * (
        grad_norm
        - jnp.mean(grad_norm, axis=-1, keepdims=True)
        - normal * jnp.mean(grad_norm * normal, axis=-1, keepdims=True)
    )
    return (grad_in, jnp.sum(grad_out * normal, axis=0), jnp.sum(grad_out, axis=0))


def swish_grad(values):
    sigmoid_val = jax.nn.sigmoid(values)
    return sigmoid_val * (1.0 + values * (1.0 - sigmoid_val))


def sinusoid(distance, feat_width):
    half_width = feat_width // 2
    inv_freq = jnp.exp(jnp.arange(half_width, dtype=f32) * (-2.0 * math.log(10000.0) / feat_width))
    angles = distance[:, None] * inv_freq[None, :]
    return jnp.concatenate([jnp.sin(angles), jnp.cos(angles)], axis=1)


class Layout:
    def __init__(self, utt_count):
        self.dp, self.tm, self.utt = lax.axis_size("dp"), lax.axis_size("tm"), utt_count
        self.pairs = self.dp // 2
        self.size = self.tm // utt_count
        self.subs = self.size // 2
        dp_at, t = lax.axis_index("dp"), lax.axis_index("tm")
        self.core, self.t = dp_at % 2, t
        group, self.sub = t // self.subs, t % self.subs
        self.home_core, self.home_slot = group % 2, group // 2
        self.own = self.core * self.subs + self.sub

    def route(self, target):
        pairs = []
        for p in range(self.pairs):
            for c in range(2):
                for t in range(self.tm):
                    tp, tc, tt = target(p, c, t)
                    pairs.append(((2 * p + c) * self.tm + t, (2 * tp + tc) * self.tm + tt))
        return pairs

    def send(self, values, target):
        return lax.ppermute(values, AXES, self.route(target))

    def to_class(self, step):
        def target(p, c, t):
            other = (c * self.subs + t % self.subs) ^ step
            return p, other // self.subs, t - t % self.subs + other % self.subs

        return target

    def to_core(self, p, c, t):
        return p, 1 - c, t

    def home(self, step):
        def target(p, c, t):
            kind, at = t // self.utt, t % self.utt
            place = (step + at) % self.utt
            return p, kind // self.subs, (2 * place + c) * self.subs + kind % self.subs

        return target

    def enter(self, shard, step):
        at = (step + self.t % self.utt) % self.utt
        block = lax.dynamic_index_in_dim(shard, at, 0, keepdims=True)
        return self.send(block, self.home(step))

    def entered(self, blocks):
        result = jnp.zeros((self.utt,) + blocks[0].shape[1:], blocks[0].dtype)
        for k, block in enumerate(blocks):
            result = lax.dynamic_update_slice_in_dim(
                result, block, (self.home_slot - k) % self.utt, axis=0
            )
        return result

    def leave(self, blocks):
        received = []
        for k in range(self.utt):
            block = lax.dynamic_index_in_dim(
                blocks, (self.home_slot - k) % self.utt, 0, keepdims=True
            )
            there = self.route(self.home(k))
            received.append(lax.ppermute(block, AXES, [(b, a) for a, b in there]))
        return received

    def left(self, received):
        at = self.t % self.utt
        result = jnp.zeros((self.utt,) + received[0].shape[1:], received[0].dtype)
        for k, block in enumerate(received):
            result = lax.dynamic_update_slice_in_dim(result, block, (k + at) % self.utt, axis=0)
        return result

    def all_slots(self, values):
        parts = [values] + [self.send(values, self.to_class(s)) for s in range(1, self.size)]
        return jnp.concatenate(parts, axis=0)

    def own_sum(self, partial):
        parts = partial.reshape((self.size, -1) + partial.shape[1:])
        total = parts[0]
        for s in range(1, self.size):
            total = total + self.send(parts[s].astype(bf16), self.to_class(s)).astype(f32)
        return total

    def over_utterances(self, values, join):
        step = 1
        groups = 2 * self.utt
        while step < self.pairs * groups:

            def target(p, c, t, step=step):
                other = (p * groups + t // self.subs) ^ step
                return other // groups, c, (other % groups) * self.subs + t % self.subs

            values = join(values, self.send(values, target))
            step *= 2
        return values

    def core_half(self, values, axis):
        shape = values.shape
        split = values.reshape(shape[:axis] + (2, shape[axis] // 2) + shape[axis + 1 :])
        return lax.dynamic_index_in_dim(split, self.core, axis, keepdims=False)

    def sub_part(self, values, axis):
        if self.subs == 1:
            return values
        width = values.shape[axis] // self.subs
        return lax.dynamic_slice_in_dim(values, self.sub * width, width, axis)

    def sub_place(self, values, axis):
        if self.subs == 1:
            return values
        width = values.shape[axis]
        shape = list(values.shape)
        shape[axis] = width * self.subs
        return lax.dynamic_update_slice_in_dim(
            jnp.zeros(shape, values.dtype), values, self.sub * width, axis
        )

    def cols_half(self, local, groups):
        rows, cols = local.shape
        split = local.reshape(rows, groups, 2, cols // (2 * groups))
        return lax.dynamic_index_in_dim(split, self.core, 2, keepdims=False).reshape(rows, cols // 2)

    def cols_join(self, halves, groups):
        _, rows, cols = halves.shape
        split = halves.reshape(2, rows, groups, cols // groups)
        return split.transpose(1, 2, 0, 3).reshape(rows, 2 * cols)

    def gather_small(self, local):
        parts = local[None]
        step = 1
        while step < self.tm:
            parts = jnp.concatenate(
                [parts, self.send(parts, lambda p, c, t, step=step: (p, c, t ^ step))], axis=0
            )
            step *= 2
        parts = jnp.take(parts, jnp.arange(self.tm, dtype=jnp.int32) ^ self.t, axis=0)
        return parts.transpose(1, 0, 2).reshape(local.shape[0], -1)

    def sum_all(self, values):
        step = 1
        while step < self.size:
            values = values + self.send(values, self.to_class(step))
            step *= 2
        return self.over_utterances(values, jnp.add)

    def gather(self, locals_, ready=None):
        plane = lax.axis_index("dp") // 2
        parts = [lax.dynamic_slice_in_dim(v, plane * (v.shape[0] // self.pairs), v.shape[0] // self.pairs, 0) for v in locals_]
        packed, places = pack(parts)
        if ready is not None:
            ready.append(packed)
        groups = [
            [(2 * p + c) * self.tm + t for t in range(self.tm) for p in range(self.pairs)]
            for c in range(2)
        ]
        full = lax.all_gather(packed[None], AXES, axis=0, tiled=True, axis_index_groups=groups)
        return [v.reshape(-1, v.shape[-1]) for v in unpack(full, places)]

    def scatter(self, grads, over_planes=False, after=None, hold=None):
        plane = lax.axis_index("dp") // 2
        split = [g.astype(bf16).reshape(self.tm, self.pairs, -1, g.shape[-1]) for g in grads]

        def part(at):
            return pack([lax.dynamic_index_in_dim(v, at, 1, keepdims=False) for v in split])

        mine, places = part(plane)
        if over_planes:
            for s in range(1, self.pairs):
                other = self.send(part(plane ^ s)[0], lambda p, c, t, s=s: (p ^ s, c, t))
                mine = (mine.astype(f32) + other.astype(f32)).astype(bf16)
        else:
            mine = jnp.stack([part(plane ^ s)[0] for s in range(self.pairs)], axis=1)
        if hold is not None:
            mine, hold = lax.optimization_barrier((mine, hold))
        if after is not None:
            mine, _ = lax.optimization_barrier((mine, after))
        mine = lax.psum_scatter(mine, "tm", scatter_dimension=0, tiled=True)
        return (mine, places) if hold is None else (mine, places, hold)

    def collect(self, mine, places):
        plane = lax.axis_index("dp") // 2
        if mine.ndim == 4:
            parts = mine
            mine = parts[:, 0].astype(f32)
            for s in range(1, self.pairs):
                mine = mine + self.send(parts[:, s], lambda p, c, t, s=s: (p ^ s, c, t)).astype(f32)
            mine = mine.astype(bf16)
        whole = jnp.zeros((self.pairs,) + mine.shape[1:], bf16)
        whole = lax.dynamic_update_slice_in_dim(whole, mine, plane, 0)
        for s in range(1, self.pairs):
            other = self.send(mine, lambda p, c, t, s=s: (p ^ s, c, t))
            whole = lax.dynamic_update_slice_in_dim(whole, other, plane ^ s, 0)
        there = self.send(whole, self.to_core)
        both = jnp.stack(
            [jnp.where(self.core == 0, whole, there), jnp.where(self.core == 0, there, whole)]
        )
        return [v.astype(f32).reshape(2, -1, v.shape[-1]) for v in unpack(both, places)]


def pack(parts):
    blocks, places, row, spare = [], [], 0, None
    for v in parts:
        rows, cols, own = v.shape[-2], v.shape[-1], []
        for at in range(0, cols - D + 1, D):
            blocks.append([v[..., at : at + D]])
            own.append((row, 0, rows, D))
            row += rows
        if cols % D:
            piece = v[..., cols - cols % D :]
            if spare is not None and spare[1] == rows and spare[2] + cols % D <= D:
                blocks[spare[0]].append(piece)
                own.append((spare[3], spare[2], rows, cols % D))
                spare = None
            else:
                spare = (len(blocks), rows, cols % D, row)
                blocks.append([piece])
                own.append((row, 0, rows, cols % D))
                row += rows
        places.append(own)
    filled = []
    for block in blocks:
        joined = block[0] if len(block) == 1 else jnp.concatenate(block, axis=-1)
        if joined.shape[-1] < D:
            pads = [(0, 0)] * (joined.ndim - 1) + [(0, D - joined.shape[-1])]
            joined = jnp.pad(joined, pads)
        filled.append(joined)
    return jnp.concatenate(filled, axis=-2), places


def unpack(packed, places):
    results = []
    for own in places:
        pieces = [packed[..., r : r + n, c : c + m] for r, c, n, m in own]
        results.append(pieces[0] if len(pieces) == 1 else jnp.concatenate(pieces, axis=-1))
    return results


def merge_moments(left, right):
    count_a, mean_a, square_a = left[0], left[1], left[2]
    count_b, mean_b, square_b = right[0], right[1], right[2]
    count = count_a + count_b
    gap = mean_a - mean_b
    mean = (count_a * mean_a + count_b * mean_b) / count
    square = (square_a + square_b) + gap * gap * (count_a * count_b / count)
    return jnp.stack([count, mean, square])


def body(
    inputs,
    cotangent,
    lengths,
    first_up,
    first_down,
    joint_proj,
    rel_proj,
    merge_proj,
    conv_wide,
    conv_narrow,
    second_up,
    second_down,
    norm_gains,
    norm_shifts,
    pos_biases,
    depth_taps,
):
    lay = Layout(inputs.shape[0])
    utt_count, block_len, _ = inputs.shape
    tm, size, own = lay.tm, lay.size, lay.own
    rows = utt_count * block_len
    span = rows * size
    feats = D // size
    pad_width = KW // 2

    def own_feats(values):
        count = values.shape[0]
        split = values.reshape(count, tm, 2, D // (2 * tm))
        half = lax.dynamic_index_in_dim(split, lay.core, 2, keepdims=False)
        return lay.sub_part(half.reshape(count, D // 2), 1)

    def place_feats(values):
        count = values.shape[0]
        half = lay.sub_place(values, 1).reshape(count, tm, 1, D // (2 * tm))
        pick = (jnp.arange(2) == lay.core).astype(f32)[None, None, :, None]
        return (half * pick).reshape(count, D)

    def place_heads(values):
        return lax.dynamic_update_slice_in_dim(
            jnp.zeros((values.shape[0], D), f32), values, own * feats, axis=1
        )

    ready = []
    up_one, down_one, joint_half, rel_half = lay.gather(
        [
            lay.cols_half(first_up, tm),
            lay.core_half(first_down, 0),
            lay.cols_half(joint_proj, 3),
            lay.cols_half(rel_proj, 1),
        ],
        ready,
    )
    _, inputs, norm_gains = lax.optimization_barrier((ready[0], inputs, norm_gains))
    small = jnp.concatenate([norm_gains, norm_shifts, pos_biases, depth_taps], axis=0)
    small = lay.gather_small(small).astype(f32)
    gain_rows, shift_rows = small[0:6], small[6:12]

    bias_rows = lax.dynamic_slice_in_dim(small[12:14], own * feats, feats, axis=1)
    kernel_taps = own_feats(small[14 : 14 + KW])
    batch_gain, batch_shift = own_feats(gain_rows[5:6])[0], own_feats(shift_rows[5:6])[0]

    merge_full, wide_half, narrow_half, up_two, down_two = lay.gather(
        [
            merge_proj,
            lay.cols_half(conv_wide, 2 * tm),
            lay.core_half(conv_narrow, 0),
            lay.cols_half(second_up, tm),
            lay.core_half(second_down, 0),
        ]
    )
    up_one, down_one = lay.sub_part(up_one, 1), lay.sub_part(down_one, 0)
    up_two, down_two = lay.sub_part(up_two, 1), lay.sub_part(down_two, 0)
    joint_own = lay.sub_part(joint_half.reshape(D, 3, D // 2), 2).reshape(D, 3 * feats)
    rel_own = lay.sub_part(rel_half, 1)
    wide_own = lay.sub_part(wide_half.reshape(D, 2, D // 2), 2).reshape(D, 2 * feats)
    narrow_own = lay.sub_part(narrow_half, 0)
    def feed_forward(values, gain_row, shift_row, up_weight, down_weight):
        normed, normal, scale_inv = norm_fwd(values, gain_row, shift_row)
        normed_low = lay.all_slots(normed.astype(bf16))
        hidden = product(normed_low, up_weight)
        active_low = (hidden * jax.nn.sigmoid(hidden)).astype(bf16)
        result = lay.own_sum(product(active_low, down_weight))
        return (result, (normal, scale_inv, normed_low, hidden, active_low))

    def feed_back(grad_result, saved_acts, gain_row, up_weight, down_weight, between):
        normal, scale_inv, normed_low, hidden, active_low = saved_acts
        grad_low = lay.all_slots(grad_result.astype(bf16))
        grad_down = product_tn(active_low, grad_low).astype(bf16)
        grad_down, grad_low = lax.optimization_barrier((grad_down, grad_low))
        grad_hidden = (product_nt(grad_low, down_weight) * swish_grad(hidden)).astype(bf16)
        grad_up = product_tn(normed_low, grad_hidden).astype(bf16)
        grad_down, grad_up = lay.sub_place(grad_down, 0), lay.sub_place(grad_up, 1)
        grad_hidden, moved = between(grad_down, grad_up, grad_hidden)
        grad_values, grad_gain, grad_shift = norm_back(
            lay.own_sum(product_nt(grad_hidden, up_weight)), normal, scale_inv, gain_row
        )
        return (grad_values, moved, grad_gain, grad_shift)

    group_lengths = jnp.where(
        lay.home_core == lay.core, lengths, lay.send(lengths, lay.to_core)
    )
    length = lax.dynamic_index_in_dim(group_lengths, lay.home_slot, 0, keepdims=False)
    slot_class = jnp.arange(size, dtype=jnp.int32) ^ own
    frame_pos = slot_class[:, None] * rows + jnp.arange(rows, dtype=jnp.int32)[None, :]
    live = frame_pos < length
    live_col = live.astype(f32)[:, :, None]
    key_mask = jnp.where(live, 0.0, neg_fill).astype(f32)
    key_extra = jnp.where(
        jnp.arange(HEAD_DIM) == 0, key_mask[:, :, None], 1.0
    ).astype(bf16)
    own_at = own.reshape(1).astype(jnp.int32)

    def framed_rows(values):
        last, leading = values[:, rows - pad_width :], values[:, :pad_width]
        before, after = [], []
        for s in range(size):
            kind = own ^ s
            prev = lax.dynamic_index_in_dim(last, jnp.maximum(kind - 1, 0) ^ own, 0)
            following = lax.dynamic_index_in_dim(
                leading, jnp.minimum(kind + 1, size - 1) ^ own, 0
            )
            before.append(jnp.where(kind > 0, prev, 0.0))
            after.append(jnp.where(kind < size - 1, following, 0.0))
        return jnp.concatenate(
            [jnp.concatenate(before, axis=0), values, jnp.concatenate(after, axis=0)], axis=1
        )

    distance = (span - 1 - jnp.arange(2 * span, dtype=jnp.int32)).astype(f32)
    table_low = sinusoid(distance, D).astype(bf16)
    up_one, table_low = lax.optimization_barrier((up_one, table_low))
    steps = range(utt_count)
    section_zero = lay.entered([lay.enter(inputs, k) for k in steps]).astype(f32).reshape(rows, D)
    branch_one, saved_one = feed_forward(
        section_zero, gain_rows[0], shift_rows[0], up_one, down_one
    )
    section_one = section_zero + 0.5 * branch_one
    att_normed, att_normal, att_inv = norm_fwd(section_one, gain_rows[1], shift_rows[1])
    att_low = lay.all_slots(att_normed.astype(bf16))
    joint_out = product(att_low, joint_own).astype(bf16).reshape(size, rows, 3 * feats)
    rel_low = product(table_low, rel_own).astype(bf16)
    attended, log_totals = attend(
        own_at, joint_out, rel_low, bias_rows, key_mask.reshape(1, span)
    )

    merge_full, cotangent = lax.optimization_barrier((merge_full, cotangent))
    entries = [lay.enter(cotangent, k) for k in steps]
    merge_slots = jnp.concatenate(
        [
            lax.dynamic_slice_in_dim(merge_full, (own ^ s) * feats, feats, axis=0)
            for s in range(size)
        ],
        axis=0,
    )
    attended_low = jnp.concatenate(
        [attended[0]] + [lay.send(attended[s], lay.to_class(s)) for s in range(1, size)], axis=1
    )
    section_two = section_one + product(attended_low, merge_slots)
    conv_normed, conv_normal, conv_inv = norm_fwd(section_two, gain_rows[2], shift_rows[2])
    conv_low = lay.all_slots(conv_normed.astype(bf16))
    wide_out = product(conv_low, wide_own).reshape(size, rows, 2 * feats)
    lin_half = wide_out[:, :, :feats]
    gate_sig = jax.nn.sigmoid(wide_out[:, :, feats:])
    gated = lin_half * gate_sig * live_col
    framed = framed_rows(gated)
    depth_out = kernel_taps[0] * framed[:, 0:rows]
    for offset in range(1, KW):
        depth_out = depth_out + kernel_taps[offset] * framed[:, offset : offset + rows]
    own_count = length.astype(f32)
    own_mean = jnp.sum(depth_out * live_col, axis=(0, 1)) / own_count
    own_gap = (depth_out - own_mean) * live_col
    moments = jnp.stack(
        [jnp.broadcast_to(own_count, (feats,)), own_mean, jnp.sum(own_gap * own_gap, axis=(0, 1))]
    )
    moments, entries = lax.optimization_barrier((moments, entries))
    total_count, bn_mean, total_var = lay.over_utterances(moments, merge_moments)
    bn_inv = lax.rsqrt(total_var / total_count + eps_norm)
    bn_normal = (depth_out - bn_mean) * bn_inv
    bn_flat = bn_normal * batch_gain + batch_shift
    swish_low = (bn_flat * jax.nn.sigmoid(bn_flat)).astype(bf16).reshape(span, feats)
    section_three = section_two + lay.own_sum(product(swish_low, narrow_own))
    branch_four, saved_four = feed_forward(
        section_three, gain_rows[3], shift_rows[3], up_two, down_two
    )
    section_four = section_three + 0.5 * branch_four
    final_out, final_normal, final_inv = norm_fwd(section_four, gain_rows[4], shift_rows[4])
    final_low = final_out.astype(bf16).reshape(utt_count, block_len, D)

    grad_final = lay.entered(entries).astype(f32).reshape(rows, D)
    grad_four, gain_four, shift_four = norm_back(grad_final, final_normal, final_inv, gain_rows[4])

    def scatter_two(grad_down, grad_up, grad_hidden):
        grad_up, grad_hidden = lax.optimization_barrier((grad_up, grad_hidden))
        return grad_hidden, (lay.scatter([grad_up]), lay.scatter([grad_down]))

    grad_mid, (moved_up_two, moved_down_two), gain_three, shift_three = feed_back(
        0.5 * grad_four, saved_four, gain_rows[3], up_two, down_two, scatter_two
    )
    grad_three = grad_four + grad_mid
    narrow_low = lay.all_slots(grad_three.astype(bf16))
    grad_narrow = lay.sub_place(product_tn(swish_low, narrow_low), 0)
    grad_batch = product_nt(narrow_low, narrow_own).reshape(size, rows, feats) * swish_grad(bn_flat)
    gain_batch = jnp.sum(grad_batch * bn_normal, axis=(0, 1))
    shift_batch = jnp.sum(grad_batch, axis=(0, 1))
    grad_hat = grad_batch * batch_gain
    total_hat, total_cross = lay.over_utterances(
        jnp.stack([shift_batch * batch_gain, gain_batch * batch_gain]), jnp.add
    )
    grad_depth = bn_inv * (
        grad_hat - live_col / total_count * (total_hat + bn_normal * total_cross)
    )
    grad_framed = framed_rows(grad_depth)
    grad_gated = kernel_taps[0] * grad_framed[:, KW - 1 : KW - 1 + rows]
    for offset in range(1, KW):
        grad_gated = (
            grad_gated + kernel_taps[offset] * grad_framed[:, KW - 1 - offset : KW - 1 - offset + rows]
        )
    grad_taps = jnp.stack(
        [
            jnp.sum(grad_depth * framed[:, offset : offset + rows], axis=(0, 1))
            for offset in range(KW)
        ]
    )
    grad_glu = grad_gated * live_col
    grad_wide_out = (
        jnp.concatenate(
            [grad_glu * gate_sig, grad_glu * lin_half * gate_sig * (1.0 - gate_sig)], axis=2
        )
        .astype(bf16)
        .reshape(span, 2 * feats)
    )
    grad_wide = lay.sub_place(product_tn(conv_low, grad_wide_out).reshape(D, 2, feats), 2)
    grad_conv_in, gain_two, shift_two = norm_back(
        lay.own_sum(product_nt(grad_wide_out, wide_own)), conv_normal, conv_inv, gain_rows[2]
    )
    grad_two = grad_three + grad_conv_in
    merge_low = grad_two.astype(bf16)
    grad_merge = product_tn(attended_low, merge_low).astype(bf16)
    grad_merge = jnp.concatenate(
        [
            lax.dynamic_slice_in_dim(grad_merge, (own ^ s) * feats, feats, axis=0)
            for s in range(size)
        ],
        axis=0,
    )
    halves = grad_merge.reshape(D, 2, D // 2)
    mine = lax.dynamic_index_in_dim(halves, lay.core, 1, keepdims=False)
    theirs = lax.dynamic_index_in_dim(halves, 1 - lay.core, 1, keepdims=False)
    grad_merge = mine.astype(f32) + lay.send(theirs, lay.to_core).astype(f32)
    grad_attended = product_nt(merge_low, merge_slots).astype(bf16).reshape(rows, size, feats)
    grad_attended = jnp.stack(
        [grad_attended[:, 0]]
        + [lay.send(grad_attended[:, s], lay.to_class(s)) for s in range(1, size)]
    )
    grad_attended, final_low = lax.optimization_barrier((grad_attended, final_low))
    output = lay.leave(final_low)
    moved_conv = lay.scatter([grad_merge, grad_wide.reshape(D, D), grad_narrow])
    grad_query, grad_key, grad_value, grad_rel, grad_biases = attend_back(
        own_at, joint_out, rel_low, bias_rows, key_extra, attended, grad_attended, log_totals
    )
    grad_query, rows_up_two, rows_down_two, rows_conv, output = lax.optimization_barrier(
        (grad_query, moved_up_two[0], moved_down_two[0], moved_conv[0], output)
    )
    grad_biases = grad_biases.transpose(1, 0, 2).reshape(2, feats)
    grad_joint_out = jnp.concatenate([grad_query, grad_key, grad_value], axis=2).reshape(
        span, 3 * feats
    )
    grad_joint = lay.sub_place(product_tn(att_low, grad_joint_out).reshape(D, 3, feats), 2)
    *moved_joint, grad_joint_out = lay.scatter(
        [grad_joint.reshape(D, 3 * D // 2)], hold=grad_joint_out
    )
    rel_high = grad_rel.astype(bf16)
    rel_rest = (grad_rel - rel_high.astype(f32)).astype(bf16)
    grad_rel_proj = lay.sub_place(
        product_tn(table_low, rel_high) + product_tn(table_low, rel_rest), 1
    )
    grad_att_in, gain_one, shift_one = norm_back(
        lay.own_sum(product_nt(grad_joint_out, joint_own)), att_normal, att_inv, gain_rows[1]
    )
    grad_one = grad_two + grad_att_in
    earlier = (rows_up_two, rows_down_two, rows_conv, output)

    def scatter_one(grad_down, grad_up, grad_hidden):
        grad_hidden, rows_joint = lax.optimization_barrier((grad_hidden, moved_joint[0]))
        moved_down = lay.scatter([grad_down], after=rows_joint)
        moved_up = lay.scatter([grad_up, grad_rel_proj], over_planes=True, after=moved_down[0])
        late, _ = lax.optimization_barrier((earlier + (rows_joint,), grad_up))
        return grad_hidden, (moved_down, moved_up, late)

    grad_first, (moved_down, moved_up, late), gain_zero, shift_zero = feed_back(
        0.5 * grad_one, saved_one, gain_rows[0], up_one, down_one, scatter_one
    )
    grad_zero = grad_one + grad_first
    grad_inputs = lay.left(lay.leave(grad_zero.astype(bf16).reshape(utt_count, block_len, D)))

    rows_up_two, rows_down_two, rows_conv, output, rows_joint = late
    output = lay.left(output)
    (summed_up_two,) = lay.collect(rows_up_two, moved_up_two[1])
    (summed_down_two,) = lay.collect(rows_down_two, moved_down_two[1])
    summed_merge, summed_wide, summed_narrow = lay.collect(rows_conv, moved_conv[1])
    (summed_joint,) = lay.collect(rows_joint, moved_joint[1])
    (summed_down_one,) = lay.collect(*moved_down)
    summed_up_one, summed_rel = lay.collect(*moved_up)
    summed_up_one = lay.cols_join(summed_up_one, tm)
    summed_up_two = lay.cols_join(summed_up_two, tm)
    summed_joint = lay.cols_join(summed_joint, 3)
    summed_rel = lay.cols_join(summed_rel, 1)
    summed_merge = lay.cols_join(summed_merge, 1)
    summed_wide = lay.cols_join(summed_wide, 2 * tm)
    summed_down_one = summed_down_one.reshape(-1, D)
    summed_down_two = summed_down_two.reshape(-1, D)
    summed_narrow = summed_narrow.reshape(-1, D)

    small_grads = jnp.concatenate(
        [
            jnp.stack([gain_zero, gain_one, gain_two, gain_three, gain_four]),
            place_feats(gain_batch[None]),
            jnp.stack([shift_zero, shift_one, shift_two, shift_three, shift_four]),
            place_feats(shift_batch[None]),
            place_heads(grad_biases),
            place_feats(grad_taps),
        ],
        axis=0,
    )
    small_grads = lay.sum_all(small_grads)
    small_grads = lax.dynamic_slice_in_dim(small_grads, lay.t * (D // tm), D // tm, axis=1)
    return (
        output,
        grad_inputs,
        summed_up_one,
        summed_down_one,
        summed_joint,
        summed_rel,
        summed_merge,
        summed_wide,
        summed_narrow,
        summed_up_two,
        summed_down_two,
        small_grads[0:6],
        small_grads[6:12],
        small_grads[12:14],
        small_grads[14 : 14 + KW],
    )


def solution(mesh):
    frames = P("dp", "tm", None)
    rows, cols = P("tm", None), P(None, "tm")
    return jax.shard_map(
        body,
        mesh=mesh,
        in_specs=(frames, frames, P("dp")) + (rows,) * 9 + (cols,) * 4,
        out_specs=(frames, frames) + (rows,) * 9 + (cols,) * 4,
        check_vma=False,
    )
```
